512 devices in a mesh: rows: 16 (over z_lo, x), cols: 32 (over y, z_hi, core).
Axes of the slice: x: 4, y: 4, z: 16 (z_hi: 4, z_lo: 4; z = z_hi * 4 + z_lo), core: 2. Of those that a mesh axis runs over, the one named last changes fastest.
Arguments:
- file_pixels: bfloat16 [48, 512, 4096], P(None, ('rows', 'cols')), may hold values from -6 to 6
- patchify_weight: bfloat16 [64, 48], replicated, may hold values from -0.875 to 0.875
- patchify_bias: float32 [64], replicated, may hold values from -3 to 3
- norm_gain: float32 [64], replicated, may hold values from 0.5 to 1.5
- norm_offset_vector: float32 [64], replicated, may hold values from -3 to 3
- kernel: float32 [64, 49], replicated, may hold values from -0.875 to 0.875
- kernel_offset: float32 [64], replicated, may hold values from -3 to 3
- cotangent: bfloat16 [64, 512, 4096], P(None, 'rows', 'cols'), may hold values from -10 to 10, as said below
Outputs:
- stem_output: bfloat16 [64, 512, 4096], P(None, 'rows', 'cols')
- weight_grad: float32 [64, 48], replicated
- bias_grad: float32 [64], replicated
- norm_scale_gradient: float32 [64], replicated
- shift_grad: float32 [64], replicated
- kernel_grad: float32 [64, 49], replicated
- offset_grad: float32 [64], replicated
The draws below stay inside these ranges and needn't reach their ends.
Inputs may be any that keep to these rules, and one draw needn't show every extreme that they name: A cotangent of order one.
All inputs are finite; a program needn't handle non-finite values.
Results may differ from the reference program's by a relative error of at most 0.0055.
Values may be sent and summed in bfloat16 or wider, within the bound.
A program may use at most 64 MiB of HBM per device.

```python
import math
import jax
import jax.numpy as jnp
from jax import lax

CH = 64
PIX = 48
KS = 7
H_DEV = 32
NH = 512
NW = 4096


def draw_cotangent(key, part):
    row_pos = jnp.arange(NH, dtype=jnp.float32)[:, None] / NH
    col_pos = jnp.arange(NW, dtype=jnp.float32)[None, :] / NW
    level = 0.5 + row_pos + col_pos
    base = jnp.clip(jax.random.normal(key, (CH, NH, NW), jnp.float32), -4.0, 4.0)
    return (base * level[None]).astype(jnp.bfloat16)


def steps_of(own_key, extent, split, smallest, largest):
    def one(axis_at, parts):
        heights = jax.random.uniform(jax.random.fold_in(jax.random.fold_in(own_key, 6), axis_at), (parts,), jnp.float32, smallest / len(split), largest / len(split))
        return jnp.repeat(jnp.exp(heights), extent[axis_at] // parts).reshape((-1,) + (1,) * (len(extent) - axis_at - 1))

    level = one(*split[0])
    for cut in split[1:]:
        level = level * one(*cut)
    return level


def normal_values(stream_key, dims, scale, most, pieces=(), kind=jnp.bfloat16):
    array = jax.random.normal(stream_key, dims, jnp.float32) * scale
    if len(pieces) > 0:
        array = steps_of(stream_key, dims, pieces, -0.22, 0.18) * array
    return jnp.clip(array, min=-most, max=most).astype(kind)


def setup_inputs(seed: int = 0) -> dict:
    arg_keys = jax.random.split(jax.random.key(seed), 9)
    return {
        "file_pixels": normal_values(arg_keys[0], (PIX, NH, NW), 1.0, 6.0, ((1, 512),)),
        "patchify_weight": normal_values(arg_keys[1], (CH, PIX), PIX ** -0.5, 0.875),
        "patchify_bias": normal_values(arg_keys[2], (CH,), 0.5, 3.0, (), jnp.float32),
        "norm_gain": jnp.clip(1.0 + 0.1 * jax.random.normal(arg_keys[3], (CH,), jnp.float32), 0.5, 1.5),
        "norm_offset_vector": normal_values(arg_keys[4], (CH,), 0.5, 3.0, (), jnp.float32),
        "kernel": normal_values(arg_keys[5], (CH, KS * KS), (KS * KS) ** -0.5, 0.875, (), jnp.float32),
        "kernel_offset": normal_values(arg_keys[6], (CH,), 0.5, 3.0, (), jnp.float32),
        "cotangent": draw_cotangent(jax.random.fold_in(arg_keys[8], 71), 0),
    }


norm_eps = 1e-06

def embed_patches(pixel_values, weight, bias):
    flat = pixel_values.reshape(pixel_values.shape[0], -1)
    mixed = jnp.dot(weight, flat, preferred_element_type=jnp.float32) + bias[:, None]
    return mixed.astype(jnp.bfloat16).reshape(weight.shape[0], pixel_values.shape[1], pixel_values.shape[2])

def apply_layer_norm(patch_embedding):
    values = patch_embedding.astype(jnp.float32)
    center = values - lax.optimization_barrier(jnp.mean(values, axis=0, keepdims=True))
    spread = lax.optimization_barrier(jnp.mean(center * center, axis=0, keepdims=True))
    inverse_deviation = lax.rsqrt(spread + norm_eps)
    return (center * inverse_deviation, inverse_deviation)

def reference(file_pixels, patchify_weight, patchify_bias, norm_gain, norm_offset_vector, kernel, kernel_offset, cotangent):
    blocks = NH // H_DEV
    pix_blocks = file_pixels.reshape(PIX, blocks, H_DEV, NW).transpose(1, 0, 2, 3)
    scale_factor = norm_gain[:, None, None]
    offset_vector = norm_offset_vector[:, None, None]

    def forward_block(pixel_values):
        centered_input, inverse_deviation = apply_layer_norm(embed_patches(pixel_values, patchify_weight, patchify_bias))
        return (centered_input * scale_factor + offset_vector).astype(jnp.bfloat16)
    normalized_output = lax.map(forward_block, pix_blocks).transpose(1, 0, 2, 3).reshape(CH, NH, NW)
    factor = 1.0 / math.sqrt(NH * NW)

    def per_channel(items):
        plane, cot, taps, offset = items
        padded = jnp.pad(plane, 3)
        cot_pad = jnp.pad(cot, 3)
        upstream = cot.astype(jnp.float32) * factor
        total = jnp.zeros((NH, NW), jnp.float32) + offset
        back = jnp.zeros((NH, NW), jnp.float32)
        grads = []
        for tap_row in range(KS):
            for tap_col in range(KS):
                window = padded[tap_row:tap_row + NH, tap_col:tap_col + NW].astype(jnp.float32)
                total = total + taps[tap_row * KS + tap_col] * window
                grads.append(jnp.sum(window * upstream))
                mirror = cot_pad[6 - tap_row:6 - tap_row + NH, 6 - tap_col:6 - tap_col + NW].astype(jnp.float32)
                back = back + taps[tap_row * KS + tap_col] * mirror
        return (total.astype(jnp.bfloat16), jnp.stack(grads), jnp.sum(upstream), back * factor)
    stem_output, kernel_grad, offset_grad, normalized_gradient = lax.map(per_channel, (normalized_output, cotangent, kernel, kernel_offset))
    grad_blocks = normalized_gradient.reshape(CH, blocks, H_DEV, NW).transpose(1, 0, 2, 3)

    def backward_block(carry, items):
        pixel_values, upper_bound = items
        centered_input, inverse_deviation = apply_layer_norm(embed_patches(pixel_values, patchify_weight, patchify_bias))
        input_gradient = upper_bound * scale_factor
        patch_gradient = inverse_deviation * (input_gradient - lax.optimization_barrier(jnp.mean(input_gradient, axis=0, keepdims=True)) - centered_input * lax.optimization_barrier(jnp.mean(input_gradient * centered_input, axis=0, keepdims=True)))
        patch_gradient = patch_gradient.astype(jnp.bfloat16)
        partial_weight = lax.dot_general(patch_gradient.reshape(CH, -1), pixel_values.reshape(PIX, -1), (((1,), (1,)), ((), ())), preferred_element_type=jnp.float32)
        partial_pieces = (partial_weight, lax.optimization_barrier(jnp.sum(patch_gradient.astype(jnp.float32), axis=(1, 2))), lax.optimization_barrier(jnp.sum(upper_bound * centered_input, axis=(1, 2))), lax.optimization_barrier(jnp.sum(upper_bound, axis=(1, 2))))
        return (jax.tree.map(lambda a, b: a + b, carry, partial_pieces), None)
    start = (jnp.zeros((CH, PIX), jnp.float32), jnp.zeros((CH,), jnp.float32), jnp.zeros((CH,), jnp.float32), jnp.zeros((CH,), jnp.float32))
    sums, unused = lax.scan(backward_block, start, (pix_blocks, grad_blocks))
    weight_grad, bias_grad, norm_scale_gradient, shift_grad = sums
    return (stem_output, weight_grad, bias_grad, norm_scale_gradient, shift_grad, kernel_grad, offset_grad)
```

```python
import functools
import math

import jax
import jax.numpy as jnp
from jax import lax
from jax.experimental import pallas as pl
from jax.experimental.pallas import tpu as pltpu
from jax.sharding import PartitionSpec as P

MESH = pl.DeviceIdType.MESH
F32 = jnp.float32
BF16 = jnp.bfloat16
norm_eps = 1e-06
side = 7
reach = 3
lanes = 128
sub = 8
PLACE = {"z_lo": 4, "x": 4, "y": 4, "z_hi": 4, "core": 2}


def body(
    place,
    pix,
    cot,
    weight,
    bias,
    gain,
    shift,
    kernel,
    koff,
    stem,
    total,
    pixb,
    up,
    uph,
    nor,
    norh,
    xhat,
    inv,
    ng,
    acc,
    taps,
    cols,
    pgb,
    sums,
    urow,
    upack,
    upeer,
    prow,
    ppack,
    ppeer,
    pay,
    rs,
    part,
    ex,
    part2,
    ey,
    part3,
    tot,
    a_send,
    a_recv,
    own_sem,
    u_send,
    u_recv,
    p_send,
    p_recv,
    r_send,
    r_recv,
    e_send,
    e_recv,
    z_send,
    z_recv,
    g_send,
    g_recv,
):
    nr = place["z_lo"] * place["x"]
    nc = place["y"] * place["z_hi"] * place["core"]
    height = cot.shape[0]
    ch = cot.shape[1]
    npix = pix.shape[0]
    tall = height + 2 * reach
    groups = ch // sub
    factor = 1.0 / math.sqrt(height * nr * lanes * nc)
    row = lax.axis_index("rows")
    col = lax.axis_index("cols")
    nx, ncore, nzl, ny, nzh = (place[k] for k in ("x", "core", "z_lo", "y", "z_hi"))
    x, zl = lax.rem(row, nx), row // nx
    core = lax.rem(col, ncore)
    zh = lax.rem(col // ncore, nzh)
    y = col // (ncore * nzh)
    lane8 = lax.broadcasted_iota(jnp.int32, (sub, lanes), 1)
    lane = lax.broadcasted_iota(jnp.int32, (ch, lanes), 1)
    lanep = lax.broadcasted_iota(jnp.int32, (npix, lanes), 1)

    def at_row(step):
        return lax.rem(row + step + nr, nr)

    def at_col(step):
        return lax.rem(col + step + nc, nc)

    n1, n2, n3 = nx * ncore, ny * nzl, nzh
    me1, me2, me3 = x * ncore + core, y * nzl + zl, zh

    def peer1(m):
        return (zl * nx + m // ncore, (col - core) + lax.rem(m, ncore))

    def peer2(m):
        return (lax.rem(m, nzl) * nx + x, (m // nzl) * (ncore * nzh) + lax.rem(col, ncore * nzh))

    def peer3(m):
        return (row, y * (ncore * nzh) + m * ncore + core)

    barrier = pltpu.get_barrier_semaphore()

    def greet(device):
        pl.semaphore_signal(barrier, inc=1, device_id=device, device_id_type=MESH)

    def greet_col(d, carry):
        greet((row, at_col(d)))
        return carry

    lax.fori_loop(1, nc, greet_col, 0)
    near = [(dr, dc) for dr in (-1, 1) for dc in (-1, 0, 1)]
    for dr, dc in near:
        greet((at_row(dr), at_col(dc)))

    def greet1(d, carry):
        greet(peer1(lax.rem(me1 + d, n1)))
        return carry

    def greet2(d, carry):
        greet(peer2(lax.rem(me2 + d, n2)))
        return carry

    lax.fori_loop(1, n1, greet1, 0)
    lax.fori_loop(1, n2, greet2, 0)

    def pack(load, mask_lane, shape):
        def step(h, both):
            left, right = both
            v = load(h)
            at = 3 * h
            left = jnp.where(
                (mask_lane >= at) & (mask_lane < at + 3), pltpu.roll(v, at, 1), left
            )
            right = jnp.where(
                (mask_lane >= 125 - at) & (mask_lane < 128 - at),
                pltpu.roll(v, lanes - at, 1),
                right,
            )
            return left, right

        zero = jnp.zeros(shape, F32)
        v = load(0)
        first = (
            jnp.where(mask_lane < 3, v, zero),
            jnp.where(mask_lane >= 125, v, zero),
        )
        return lax.fori_loop(1, height, step, first)

    def lift(h, carry):
        up[h + reach] = cot[h].astype(F32)
        return carry

    lax.fori_loop(0, height, lift, 0)
    left, right = pack(lambda h: up[h + reach], lane, (ch, lanes))
    upack[0] = left.astype(BF16)
    upack[1] = right.astype(BF16)

    pl.semaphore_wait(barrier, (nc - 1) + len(near) + (n1 - 1) + (n2 - 1))

    def halo_copies(rows_lo, rows_hi, packed, row_dst, pack_dst, send, recv):
        copies = [
            pltpu.make_async_remote_copy(
                src_ref=rows_lo,
                dst_ref=row_dst.at[1],
                send_sem=send.at[0],
                recv_sem=recv.at[1],
                device_id=(at_row(-1), col),
                device_id_type=MESH,
            ),
            pltpu.make_async_remote_copy(
                src_ref=rows_hi,
                dst_ref=row_dst.at[0],
                send_sem=send.at[1],
                recv_sem=recv.at[0],
                device_id=(at_row(1), col),
                device_id_type=MESH,
            ),
        ]
        for which, dc in ((0, -1), (1, 1)):
            for dr in (0, -1, 1):
                slot = (1 - which) * 3 + (1 - dr)
                copies.append(
                    pltpu.make_async_remote_copy(
                        src_ref=packed.at[which],
                        dst_ref=pack_dst.at[slot],
                        send_sem=send.at[2 + slot],
                        recv_sem=recv.at[2 + slot],
                        device_id=(at_row(dr), at_col(dc)),
                        device_id_type=MESH,
                    )
                )
        return copies

    u_copies = halo_copies(
        cot.at[0:reach], cot.at[height - reach : height], upack, urow, upeer, u_send, u_recv
    )
    for copy in u_copies:
        copy.start()

    def block(c):
        return pl.ds(pl.multiple_of(c * lanes, lanes), lanes)

    def send_pix(d):
        target = at_col(d)
        return pltpu.make_async_remote_copy(
            src_ref=pix.at[:, block(target)],
            dst_ref=pixb.at[0:npix, block(col)],
            send_sem=a_send.at[d],
            recv_sem=a_recv.at[col],
            device_id=(row, target),
            device_id_type=MESH,
        )

    def got_pix(d):
        source = at_col(d)
        return pltpu.make_async_remote_copy(
            src_ref=pix.at[:, block(col)],
            dst_ref=pixb.at[0:npix, block(source)],
            send_sem=a_send.at[d],
            recv_sem=a_recv.at[source],
            device_id=(row, source),
            device_id_type=MESH,
        )

    def start_pix(d, carry):
        send_pix(d).start()
        return carry

    lax.fori_loop(1, nc, start_pix, 0)
    own = pltpu.make_async_copy(pix.at[:, block(col)], pixb.at[0:npix, block(col)], own_sem)
    own.start()

    eye = lax.broadcasted_iota(jnp.int32, (ch, ch), 0) == lax.broadcasted_iota(
        jnp.int32, (ch, ch), 1
    )
    for at, ref in enumerate((bias, gain, shift, koff)):
        line = jnp.broadcast_to(ref[...], (ch, ch))
        column = jnp.sum(jnp.where(eye, line, 0.0), axis=1, keepdims=True)
        cols[at] = jnp.broadcast_to(column, (ch, lanes))
    for tap in range(side * side):
        taps[tap] = jnp.broadcast_to(kernel[:, tap : tap + 1], (ch, lanes))
    extra = pixb.shape[0] - npix
    wide = pixb.shape[1]
    pixb[npix:, :] = jnp.where(
        lax.broadcasted_iota(jnp.int32, (extra, wide), 0) == 0, 1.0, 0.0
    ).astype(BF16)

    def clear(h, carry):
        ng[h] = jnp.zeros((ch, lanes), F32)
        acc[h] = cols[3]
        return carry

    lax.fori_loop(0, height, clear, 0)

    top, bottom = row > 0, row < nr - 1
    west, east = col > 0, col < nc - 1

    def spread(peer, out, width):
        for at, (first, count, rows_ok) in enumerate(
            ((height - reach, reach, top), (0, height, None), (0, reach, bottom))
        ):
            keep_l = west if rows_ok is None else west & rows_ok
            keep_r = east if rows_ok is None else east & rows_ok
            lo = jnp.where(keep_l, peer(at), 0.0)
            hi = jnp.where(keep_r, peer(3 + at), 0.0)
            base = (0, reach, reach + height)[at]

            def one(k, carry, first=first, base=base, lo=lo, hi=hi):
                h = first + k
                out[base + k] = jnp.where(
                    lane < 64,
                    pltpu.roll(hi, lax.rem(lanes - 3 * h, lanes), 1),
                    pltpu.roll(lo, 3 * h, 1),
                )
                return carry

            lax.fori_loop(0, count, one, 0)

    for copy in u_copies:
        copy.wait_recv()
    for k in range(reach):
        up[k] = jnp.where(top, urow[0, k].astype(F32), 0.0)
        up[height + reach + k] = jnp.where(bottom, urow[1, k].astype(F32), 0.0)
    spread(lambda slot: upeer[slot].astype(F32), uph, ch)

    def sweep(src, halo, out, flip, kg):
        def one(step, carry):
            g, j = step // side, lax.rem(step, side)
            gs = pl.ds(pl.multiple_of(g * sub, sub), sub)
            s = reach - j
            mask = (lane8 >= lanes - s) | (lane8 < -s)
            amount = lax.rem(s + lanes, lanes)
            if flip:
                t = [taps[(side - 1 - i) * side + (side - 1 - j), gs] for i in range(side)]
            else:
                t = [taps[i * side + j, gs] for i in range(side)]
            sumk = [None] * side
            live = {}
            us = {}
            for a in range(tall):
                v = pltpu.roll(jnp.where(mask, halo[a, gs], src[a, gs]), amount, 1)
                if a < height:
                    live[a] = out[a, gs]
                    if kg:
                        us[a] = up[a + reach, gs]
                for i in range(side):
                    h = a - i
                    if 0 <= h < height:
                        live[h] = live[h] + t[i] * v
                        if kg:
                            term = us[h] * v
                            sumk[i] = term if sumk[i] is None else sumk[i] + term
                h = a - (side - 1)
                if h >= 0:
                    out[h, gs] = live.pop(h)
                    us.pop(h, None)
            if kg:
                line = pay[gs]
                for i in range(side):
                    line = jnp.where(
                        lane8 == 64 + i * side + j,
                        jnp.sum(sumk[i], axis=1, keepdims=True) * factor,
                        line,
                    )
                pay[gs] = line
            return carry

        lax.fori_loop(0, groups * side, one, 0)

    sweep(up, uph, ng, True, False)

    def wait_pix(d, carry):
        got_pix(d).wait_recv()
        return carry

    lax.fori_loop(1, nc, wait_pix, 0)
    own.wait()
    left, right = pack(lambda h: pixb[0:npix, block(h)].astype(F32), lanep, (npix, lanes))
    ppack[0] = left.astype(BF16)
    ppack[1] = right.astype(BF16)
    p_copies = halo_copies(
        pixb.at[0:npix, 0 : reach * lanes],
        pixb.at[0:npix, (height - reach) * lanes : height * lanes],
        ppack,
        prow,
        ppeer,
        p_send,
        p_recv,
    )
    for copy in p_copies:
        copy.start()

    def embed(pixels):
        patch = jnp.dot(weight[...], pixels, preferred_element_type=F32) + cols[0]
        v = patch.astype(BF16).astype(F32)
        center = v - jnp.mean(v, axis=0, keepdims=True)
        deviation = lax.rsqrt(jnp.mean(center * center, axis=0, keepdims=True) + norm_eps)
        return center * deviation, deviation

    def finish(hat):
        return (hat * cols[1] + cols[2]).astype(BF16).astype(F32)

    sums[...] = jnp.zeros_like(sums)

    def inner(h, carry):
        hat, deviation = embed(pixb[0:npix, block(h)])
        nor[h + reach] = finish(hat)
        grad = ng[h] * factor
        sums[0] += grad * hat
        sums[1] += grad
        sums[2] += up[h + reach]
        xgrad = grad * cols[1]
        mean1 = jnp.mean(xgrad, axis=0, keepdims=True)
        mean2 = jnp.mean(xgrad * hat, axis=0, keepdims=True)
        pgb[:, block(h)] = (deviation * (xgrad - mean1 - hat * mean2)).astype(BF16)
        return carry

    lax.fori_loop(0, height, inner, 0)
    grads = lax.dot_general(
        pgb[...], pixb[...], (((1,), (1,)), ((), ())), preferred_element_type=F32
    )
    pay[...] = jnp.zeros_like(pay)
    pay[:, 0 : pixb.shape[0]] = grads

    for copy in p_copies:
        copy.wait_recv()
    for k in range(reach):
        ks = slice(k * lanes, (k + 1) * lanes)
        nor[k] = jnp.where(top, finish(embed(prow[0, :, ks])[0]), 0.0)
        nor[height + reach + k] = jnp.where(bottom, finish(embed(prow[1, :, ks])[0]), 0.0)
    spread(lambda slot: finish(embed(ppeer[slot])[0]), norh, ch)

    sweep(nor, norh, acc, False, True)

    def close(h, carry):
        stem[h] = acc[h].astype(BF16)
        return carry

    lax.fori_loop(0, height, close, 0)
    last = pay[...]
    for at, scale in ((0, 1.0), (1, 1.0), (2, factor)):
        last = jnp.where(
            lane == 64 + side * side + at,
            jnp.sum(sums[at], axis=1, keepdims=True) * scale,
            last,
        )
    pay[...] = last

    share = ch // n1

    def rows_of(m):
        return pl.ds(pl.multiple_of(m * share, share), share)

    def copy1(d):
        m = lax.rem(me1 + d, n1)
        return pltpu.make_async_remote_copy(
            src_ref=pay.at[rows_of(m)],
            dst_ref=rs.at[me1],
            send_sem=r_send.at[d],
            recv_sem=r_recv.at[me1],
            device_id=peer1(m),
            device_id_type=MESH,
        )

    def got1(d):
        m = lax.rem(me1 + d, n1)
        return pltpu.make_async_remote_copy(
            src_ref=pay.at[rows_of(m)],
            dst_ref=rs.at[m],
            send_sem=r_send.at[d],
            recv_sem=r_recv.at[m],
            device_id=peer1(m),
            device_id_type=MESH,
        )

    def exchange(source, slots, me, n, peer, send, recv):
        def put(d):
            m = lax.rem(me + d, n)
            return pltpu.make_async_remote_copy(
                src_ref=source,
                dst_ref=slots.at[me],
                send_sem=send.at[d],
                recv_sem=recv.at[me],
                device_id=peer(m),
                device_id_type=MESH,
            )

        def got(d):
            m = lax.rem(me + d, n)
            return pltpu.make_async_remote_copy(
                src_ref=source,
                dst_ref=slots.at[m],
                send_sem=send.at[d],
                recv_sem=recv.at[m],
                device_id=peer(m),
                device_id_type=MESH,
            )

        def start(d, carry):
            put(d).start()
            return carry

        def arrive(d, carry):
            got(d).wait_recv()
            return carry

        def sent(d, carry):
            put(d).wait_send()
            return carry

        lax.fori_loop(1, n, start, 0)
        slots[me] = source[...]
        lax.fori_loop(1, n, arrive, 0)
        return lambda: lax.fori_loop(1, n, sent, 0)

    def start1(d, carry):
        copy1(d).start()
        return carry

    def arrive1(d, carry):
        got1(d).wait_recv()
        return carry

    def sent1(d, carry):
        copy1(d).wait_send()
        return carry

    lax.fori_loop(1, n1, start1, 0)
    rs[me1] = pay[rows_of(me1)]
    lax.fori_loop(1, n1, arrive1, 0)

    def sum_of(slots, n):
        whole = slots[0]
        for k in range(1, n):
            whole = whole + slots[k]
        return whole

    part[...] = sum_of(rs, n1)
    done2 = exchange(part, ex, me2, n2, peer2, e_send, e_recv)
    part2[...] = sum_of(ex, n2)
    done3 = exchange(part2, ey, me3, n3, peer3, z_send, z_recv)
    part3[...] = sum_of(ey, n3)
    done4 = exchange(part3, tot, me1, n1, peer1, g_send, g_recv)
    for k in range(n1):
        total[k * share : (k + 1) * share, :] = tot[k]

    def sent_pix(d, carry):
        send_pix(d).wait_send()
        return carry

    lax.fori_loop(1, nc, sent_pix, 0)
    for copy in u_copies + p_copies:
        copy.wait_send()
    lax.fori_loop(1, n1, sent1, 0)
    done2()
    done3()
    done4()


def per_device(
    place,
    file_pixels,
    patchify_weight,
    patchify_bias,
    norm_gain,
    norm_offset_vector,
    kernel,
    kernel_offset,
    cotangent,
):
    ch, height, breadth = cotangent.shape
    npix = file_pixels.shape[0]
    nc = place["y"] * place["z_hi"] * place["core"]
    n1, n2, n3 = place["x"] * place["core"], place["y"] * place["z_lo"], place["z_hi"]
    share = ch // n1
    wide = nc * lanes
    tall = height + 2 * reach
    plane = (ch, lanes)
    vmem = pl.BlockSpec(memory_space=pltpu.VMEM)
    dma = pltpu.SemaphoreType.DMA
    scratch = [
        pltpu.VMEM((64, wide), BF16),
        pltpu.VMEM((tall,) + plane, F32),
        pltpu.VMEM((tall,) + plane, F32),
        pltpu.VMEM((tall,) + plane, F32),
        pltpu.VMEM((tall,) + plane, F32),
        pltpu.VMEM((1,) + plane, F32),
        pltpu.VMEM((sub, lanes), F32),
        pltpu.VMEM((height,) + plane, F32),
        pltpu.VMEM((height,) + plane, F32),
        pltpu.VMEM((side * side,) + plane, F32),
        pltpu.VMEM((4,) + plane, F32),
        pltpu.VMEM((ch, wide), BF16),
        pltpu.VMEM((3,) + plane, F32),
        pltpu.VMEM((2, reach) + plane, BF16),
        pltpu.VMEM((2,) + plane, BF16),
        pltpu.VMEM((6,) + plane, BF16),
        pltpu.VMEM((2, npix, reach * lanes), BF16),
        pltpu.VMEM((2, npix, lanes), BF16),
        pltpu.VMEM((6, npix, lanes), BF16),
        pltpu.VMEM(plane, F32),
        pltpu.VMEM((n1, share, lanes), F32),
        pltpu.VMEM((share, lanes), F32),
        pltpu.VMEM((n2, share, lanes), F32),
        pltpu.VMEM((share, lanes), F32),
        pltpu.VMEM((n3, share, lanes), F32),
        pltpu.VMEM((share, lanes), F32),
        pltpu.VMEM((n1, share, lanes), F32),
        dma((nc,)),
        dma((nc,)),
        dma(()),
        dma((8,)),
        dma((8,)),
        dma((8,)),
        dma((8,)),
        dma((n1,)),
        dma((n1,)),
        dma((n2,)),
        dma((n2,)),
        dma((n3,)),
        dma((n3,)),
        dma((n1,)),
        dma((n1,)),
    ]
    stem, total = pl.pallas_call(
        functools.partial(body, place),
        out_shape=(
            jax.ShapeDtypeStruct((height,) + plane, BF16),
            jax.ShapeDtypeStruct(plane, F32),
        ),
        in_specs=[vmem] * 8,
        out_specs=(vmem, vmem),
        scratch_shapes=scratch,
        compiler_params=pltpu.CompilerParams(
            collective_id=0, has_side_effects=True, vmem_limit_bytes=40 << 20
        ),
    )(
        file_pixels.reshape(npix, wide),
        jnp.transpose(cotangent, (1, 0, 2)),
        patchify_weight,
        patchify_bias.reshape(1, ch),
        norm_gain.reshape(1, ch),
        norm_offset_vector.reshape(1, ch),
        kernel,
        kernel_offset.reshape(1, ch),
    )
    taps_at = 64
    after = taps_at + side * side
    return (
        jnp.transpose(stem, (1, 0, 2)),
        total[:, 0:npix],
        total[:, npix],
        total[:, after],
        total[:, after + 1],
        total[:, taps_at:after],
        total[:, after + 2],
    )


def solution(mesh, place=PLACE):
    return jax.shard_map(
        functools.partial(per_device, place),
        mesh=mesh,
        in_specs=(
            P(None, ("rows", "cols"), None),
            P(),
            P(),
            P(),
            P(),
            P(),
            P(),
            P(None, "rows", "cols"),
        ),
        out_specs=(P(None, "rows", "cols"), P(), P(), P(), P(), P(), P()),
        check_vma=False,
    )
```

```python
import functools
import math

import jax
import jax.numpy as jnp
from jax import lax
from jax.experimental import pallas as pl
from jax.experimental.pallas import tpu as pltpu
from jax.sharding import PartitionSpec as P

MESH = pl.DeviceIdType.MESH
F32 = jnp.float32
BF16 = jnp.bfloat16
norm_eps = 1e-06
side = 7
reach = 3
lanes = 128
sub = 8
PLACE = {"z_lo": 4, "x": 4, "y": 4, "z_hi": 4, "core": 2}


def body(
    place,
    pix,
    cot_in,
    weight_in,
    bias_in,
    gain_in,
    shift_in,
    kernel_in,
    koff_in,
    stem,
    total,
    cot,
    weight_t,
    lines,
    kernel,
    weight,
    cotf,
    pixb,
    up,
    uph,
    nor,
    norh,
    ng,
    acc,
    kgacc,
    taps,
    cols,
    pgb,
    sums,
    uedge,
    urow,
    upk,
    upack,
    upeer,
    prow,
    ppack,
    ppeer,
    pnk,
    turns,
    pay,
    rs,
    part,
    ex,
    part2,
    ey,
    part3,
    tot,
    pay_out,
    in_sem,
    a_send,
    a_recv,
    own_sem,
    u_send,
    u_recv,
    p_send,
    p_recv,
    r_send,
    r_recv,
    e_send,
    e_recv,
    z_send,
    z_recv,
    g_send,
    g_recv,
):
    nr = place["z_lo"] * place["x"]
    nc = place["y"] * place["z_hi"] * place["core"]
    ch, height = cot.shape[0], cot.shape[1]
    npix = pix.shape[0]
    tall = height + 2 * reach
    groups = ch // sub
    factor = 1.0 / math.sqrt(height * nr * lanes * nc)
    row = lax.axis_index("rows")
    col = lax.axis_index("cols")
    nx, ncore, nzl, ny, nzh = (place[k] for k in ("x", "core", "z_lo", "y", "z_hi"))
    x, zl = lax.rem(row, nx), row // nx
    core = lax.rem(col, ncore)
    zh = lax.rem(col // ncore, nzh)
    y = col // (ncore * nzh)
    lane8 = lax.broadcasted_iota(jnp.int32, (sub, lanes), 1)
    lane = lax.broadcasted_iota(jnp.int32, (ch, lanes), 1)
    lanep = lax.broadcasted_iota(jnp.int32, (npix, lanes), 1)

    def at_row(step):
        return lax.rem(row + step + nr, nr)

    def at_col(step):
        return lax.rem(col + step + nc, nc)

    n1, n2, n3 = nx * ncore, ny * nzl, nzh
    me1, me2, me3 = x * ncore + core, y * nzl + zl, zh

    def peer1(m):
        return (zl * nx + m // ncore, (col - core) + lax.rem(m, ncore))

    def peer2(m):
        return (lax.rem(m, nzl) * nx + x, (m // nzl) * (ncore * nzh) + lax.rem(col, ncore * nzh))

    def peer3(m):
        return (row, y * (ncore * nzh) + m * ncore + core)

    loads = [
        pltpu.make_async_copy(source, target, in_sem.at[at])
        for at, (source, target) in enumerate(
            (
                (cot_in, cot),
                (kernel_in, kernel),
                (weight_in, weight_t),
                (bias_in, lines.at[0:1]),
                (gain_in, lines.at[1:2]),
                (shift_in, lines.at[2:3]),
                (koff_in, lines.at[3:4]),
            )
        )
    ]
    for copy in loads:
        copy.start()

    barrier = pltpu.get_barrier_semaphore()

    def greet(device):
        pl.semaphore_signal(barrier, inc=1, device_id=device, device_id_type=MESH)

    far = sorted(range(nzh), key=lambda d: -min(d, nzh - d))
    near_cols = ny * ncore

    def col_of(dz, e):
        return (
            lax.rem(y + e // ncore, ny) * (ncore * nzh)
            + lax.rem(zh + dz, nzh) * ncore
            + lax.rem(core + lax.rem(e, ncore), ncore)
        )

    def each_col(act):
        for dz in far:

            def one(e, carry, dz=dz):
                act(col_of(dz, e))
                return carry

            lax.fori_loop(1 if dz == 0 else 0, near_cols, one, 0)

    each_col(lambda c: greet((row, c)))
    near = [(dr, dc) for dr in (-1, 1) for dc in (-1, 0, 1)]
    for dr, dc in near:
        greet((at_row(dr), at_col(dc)))

    def greet1(d, carry):
        greet(peer1(lax.rem(me1 + d, n1)))
        return carry

    def greet2(d, carry):
        greet(peer2(lax.rem(me2 + d, n2)))
        return carry

    lax.fori_loop(1, n2, greet2, 0)
    lax.fori_loop(1, n1, greet1, 0)

    def pack(load, mask_lane, shape):
        def step(h, both):
            left, right = both
            v = load(h)
            at = 3 * h
            here = (mask_lane >= at) & (mask_lane < at + 3)
            left = jnp.where(here, pltpu.roll(v, at, 1), left)
            right = jnp.where(here, pltpu.roll(v, at + 3, 1), right)
            return left, right

        zero = jnp.zeros(shape, F32)
        return lax.fori_loop(0, height, step, (zero, zero))

    loads[0].wait()
    for k in range(ch):
        cotf[k * height : (k + 1) * height, :] = cot[k].astype(F32)

    def lift(h, carry):
        up[h + reach] = cotf[pl.ds(h, ch, stride=height), :]
        return carry

    lax.fori_loop(0, height, lift, 0)
    left, right = pack(lambda h: up[h + reach], lane, (ch, lanes))
    upk[0] = left
    upk[1] = right
    upack[0] = left.astype(BF16)
    upack[1] = right.astype(BF16)
    for k in range(reach):
        uedge[k] = up[reach + k].astype(BF16)
        uedge[reach + k] = up[height + k].astype(BF16)

    for copy in loads[1:]:
        copy.wait()
    eye = lax.broadcasted_iota(jnp.int32, (ch, ch), 0) == lax.broadcasted_iota(
        jnp.int32, (ch, ch), 1
    )

    def column(line):
        spot = jnp.where(eye, jnp.broadcast_to(line, (ch, ch)), 0.0)
        return jnp.broadcast_to(jnp.sum(spot, axis=1, keepdims=True), (ch, lanes))

    for at in range(4):
        cols[at] = column(lines[at : at + 1, :])
    weight[...] = jnp.transpose(weight_t[...].astype(F32)).astype(BF16)

    pl.semaphore_wait(barrier, (nc - 1) + len(near) + (n1 - 1) + (n2 - 1))

    def halo_copies(rows_lo, rows_hi, packed, row_dst, pack_dst, send, recv):
        copies = [
            pltpu.make_async_remote_copy(
                src_ref=rows_lo,
                dst_ref=row_dst.at[1],
                send_sem=send.at[0],
                recv_sem=recv.at[1],
                device_id=(at_row(-1), col),
                device_id_type=MESH,
            ),
            pltpu.make_async_remote_copy(
                src_ref=rows_hi,
                dst_ref=row_dst.at[0],
                send_sem=send.at[1],
                recv_sem=recv.at[0],
                device_id=(at_row(1), col),
                device_id_type=MESH,
            ),
        ]
        for which, dc in ((0, -1), (1, 1)):
            for dr in (0, -1, 1):
                slot = (1 - which) * 3 + (1 - dr)
                copies.append(
                    pltpu.make_async_remote_copy(
                        src_ref=packed.at[which],
                        dst_ref=pack_dst.at[slot],
                        send_sem=send.at[2 + slot],
                        recv_sem=recv.at[2 + slot],
                        device_id=(at_row(dr), at_col(dc)),
                        device_id_type=MESH,
                    )
                )
        return copies

    u_copies = halo_copies(
        uedge.at[0:reach], uedge.at[reach : 2 * reach], upack, urow, upeer, u_send, u_recv
    )
    for copy in u_copies:
        copy.start()

    def block(c):
        return pl.ds(pl.multiple_of(c * lanes, lanes), lanes)

    def send_pix(target):
        return pltpu.make_async_remote_copy(
            src_ref=pix.at[:, block(target)],
            dst_ref=pixb.at[0:npix, block(col)],
            send_sem=a_send.at[target],
            recv_sem=a_recv.at[col],
            device_id=(row, target),
            device_id_type=MESH,
        )

    def got_pix(source):
        return pltpu.make_async_remote_copy(
            src_ref=pix.at[:, block(col)],
            dst_ref=pixb.at[0:npix, block(source)],
            send_sem=a_send.at[source],
            recv_sem=a_recv.at[source],
            device_id=(row, source),
            device_id_type=MESH,
        )

    each_col(lambda c: send_pix(c).start())
    own = pltpu.make_async_copy(pix.at[:, block(col)], pixb.at[0:npix, block(col)], own_sem)
    own.start()

    for tap in range(side * side):
        taps[tap] = column(kernel[tap : tap + 1, :])
    extra = pixb.shape[0] - npix
    wide = pixb.shape[1]
    pixb[npix:, :] = jnp.where(
        lax.broadcasted_iota(jnp.int32, (extra, wide), 0) == 0, 1.0, 0.0
    ).astype(BF16)

    def clear(h, carry):
        ng[h] = jnp.zeros((ch, lanes), F32)
        acc[h] = cols[3]
        return carry

    lax.fori_loop(0, height, clear, 0)

    top, bottom = row > 0, row < nr - 1
    west, east = col > 0, col < nc - 1

    def join(peer, which):
        keep = (west, east)[which]
        end = 3 * height
        own = pltpu.roll(peer(3 * which + 1), 9, 1)
        above = pltpu.roll(peer(3 * which), lanes - (end - 9), 1)
        below = pltpu.roll(peer(3 * which + 2), lax.rem(end + 9, lanes), 1)
        first, middle = lane < 9, (lane >= 9) & (lane < end + 9)
        final = (lane >= end + 9) & (lane < end + 18)
        whole = jnp.where(middle & keep, own, 0.0)
        whole = jnp.where(first & (keep & top), above, whole)
        return jnp.where(final & (keep & bottom), below, whole)

    def spread(packed, out):
        lo, hi = packed[0], packed[1]
        for a in range(tall):
            out[a] = jnp.where(
                lane < 64,
                pltpu.roll(hi, (lanes - 3 * a) % lanes, 1),
                pltpu.roll(lo, 125 - 3 * a, 1),
            )

    for copy in u_copies:
        copy.wait_recv()
    for k in range(reach):
        up[k] = jnp.where(top, urow[0, k].astype(F32), 0.0)
        up[height + reach + k] = jnp.where(bottom, urow[1, k].astype(F32), 0.0)
    for which in range(2):
        pnk[which] = join(lambda slot: upeer[slot].astype(F32), which)
    spread(pnk, uph)

    def turned(j):
        s = reach - j
        return (lane8 >= lanes - s) | (lane8 < -s), lax.rem(s + lanes, lanes)

    def sweep(src, halo, out, flip, first, final):
        def one(step, carry):
            g, j = step // side, lax.rem(step, side)
            gs = pl.ds(pl.multiple_of(g * sub, sub), sub)
            mask, amount = turned(j)
            if flip:
                t = [taps[(side - 1 - i) * side + (side - 1 - j), gs] for i in range(side)]
            else:
                t = [taps[i * side + j, gs] for i in range(side)]
            live = {}
            for a in range(tall):
                v = pltpu.roll(jnp.where(mask, halo[a, gs], src[a, gs]), amount, 1)
                if a < height:
                    live[a] = out[a, gs]
                for i in range(side):
                    h = a - i
                    if 0 <= h < height:
                        live[h] = live[h] + t[i] * v
                h = a - (side - 1)
                if h >= 0:
                    out[h, gs] = live.pop(h)
            return carry

        lax.fori_loop(first * side, final * side, one, 0)

    sweep(up, uph, ng, True, 0, groups)

    def wait_pix(d, carry):
        got_pix(at_col(d)).wait_recv()
        return carry

    lax.fori_loop(1, nc, wait_pix, 0)
    own.wait()
    left, right = pack(lambda h: pixb[0:npix, block(h)].astype(F32), lanep, (npix, lanes))
    ppack[0] = left.astype(BF16)
    ppack[1] = right.astype(BF16)
    p_copies = halo_copies(
        pixb.at[0:npix, 0 : reach * lanes],
        pixb.at[0:npix, (height - reach) * lanes : height * lanes],
        ppack,
        prow,
        ppeer,
        p_send,
        p_recv,
    )
    for copy in p_copies:
        copy.start()

    def embed(pixels):
        patch = jnp.dot(weight[...], pixels, preferred_element_type=F32) + cols[0]
        v = patch.astype(BF16).astype(F32)
        center = v - jnp.mean(v, axis=0, keepdims=True)
        deviation = lax.rsqrt(jnp.mean(center * center, axis=0, keepdims=True) + norm_eps)
        return center * deviation, deviation

    def finish(hat):
        return (hat * cols[1] + cols[2]).astype(BF16).astype(F32)

    sums[...] = jnp.zeros_like(sums)

    def inner(pair, carry):
        for k in range(2):
            h = 2 * pair + k
            hat, deviation = embed(pixb[0:npix, block(h)])
            nor[h + reach] = finish(hat)
            grad = ng[h] * factor
            sums[0, k] += grad * hat
            sums[1, k] += grad
            sums[2, k] += up[h + reach]
            xgrad = grad * cols[1]
            mean1 = jnp.mean(xgrad, axis=0, keepdims=True)
            mean2 = jnp.mean(xgrad * hat, axis=0, keepdims=True)
            pgb[:, block(h)] = (deviation * (xgrad - mean1 - hat * mean2)).astype(BF16)
        return carry

    lax.fori_loop(0, height // 2, inner, 0)
    grads = lax.dot_general(
        pgb[...], pixb[...], (((1,), (1,)), ((), ())), preferred_element_type=F32
    )
    pay[...] = jnp.zeros_like(pay)
    pay[:, 0 : pixb.shape[0]] = grads

    def kg_inner(step, carry):
        g, j = step // side, lax.rem(step, side)
        gs = pl.ds(pl.multiple_of(g * sub, sub), sub)
        mask, amount = turned(j)
        sumk = [None] * side
        us = {}
        for a in range(tall - reach):
            if a < height:
                us[a] = up[a + reach, gs]
            if a >= reach:
                v = pltpu.roll(jnp.where(mask, 0.0, nor[a, gs]), amount, 1)
                for i in range(side):
                    h = a - i
                    if 0 <= h < height:
                        term = us[h] * v
                        sumk[i] = term if sumk[i] is None else sumk[i] + term
            us.pop(a - (side - 1), None)
        for i in range(side):
            kgacc[i * side + j, gs] = sumk[i]
        return carry

    lax.fori_loop(0, groups * side, kg_inner, 0)

    for copy in p_copies:
        copy.wait_recv()
    for k in range(reach):
        ks = slice(k * lanes, (k + 1) * lanes)
        nor[k] = jnp.where(top, finish(embed(prow[0, :, ks])[0]), 0.0)
        nor[height + reach + k] = jnp.where(bottom, finish(embed(prow[1, :, ks])[0]), 0.0)
    for which in range(2):
        pnk[which] = join(lambda slot: finish(embed(ppeer[slot])[0]), which)
    for at in range(3 * side):
        turns[0, at] = pltpu.roll(pnk[0], (-at) % lanes, 1)
        turns[1, at] = pltpu.roll(pnk[1], (2 - at) % lanes, 1)
    outer = [(a, i) for a in range(tall) for i in range(side) if 0 <= a - i < height]
    outer = [(a, i) for a, i in outer if a < reach or a >= height + reach]
    lane16 = lax.broadcasted_iota(jnp.int32, (2 * sub, lanes), 1)
    place3 = lax.rem(lane16, 3)

    def kg_outer(g, carry):
        gs = pl.ds(pl.multiple_of(g * 2 * sub, 2 * sub), 2 * sub)
        for j in range(side):
            s = reach - j
            v = {}
            for a in sorted({a for a, _ in outer}):
                v[a] = nor[a, gs]
                if s > 0:
                    v[a] = jnp.where(lane16 >= lanes - s, 0.0, v[a])
                if s < 0:
                    v[a] = jnp.where(lane16 < -s, 0.0, v[a])
                v[a] = pltpu.roll(v[a], s % lanes, 1)
            if s > 0:
                edge = jnp.where(place3 < s, upk[0, gs], 0.0)
            if s < 0:
                edge = jnp.where(place3 >= reach + s, upk[1, gs], 0.0)
            for i in range(side):
                whole = kgacc[i * side + j, gs]
                for a, tap_row in outer:
                    if tap_row == i:
                        whole = whole + up[a - i + reach, gs] * v[a]
                if s > 0:
                    whole = whole + edge * turns[0, 3 * i + j, gs]
                if s < 0:
                    whole = whole + edge * turns[1, 3 * i + j - 4, gs]
                kgacc[i * side + j, gs] = whole
        return carry

    lax.fori_loop(0, ch // (2 * sub), kg_outer, 0)
    ones = jnp.ones((lanes, lanes), BF16)
    for at, scale in ((0, 1.0 / factor), (1, 1.0 / factor), (2, 1.0)):
        kgacc[side * side + at] = (sums[at, 0] + sums[at, 1]) * scale
    whole = pay[...]
    for first in range(0, side * side + 3, side):
        count = min(side, side * side + 3 - first)
        value = kgacc[first : first + count].reshape(count * ch, lanes)
        high = value.astype(BF16)
        low = (value - high.astype(F32)).astype(BF16)
        lines_of = jnp.dot(high, ones, preferred_element_type=F32)
        lines_of += jnp.dot(low, ones, preferred_element_type=F32)
        for k in range(count):
            whole = jnp.where(
                lane == 64 + first + k, lines_of[k * ch : (k + 1) * ch] * factor, whole
            )
    pay[...] = whole

    def close(h, carry):
        stem[h] = acc[h].astype(BF16)
        return carry

    def piece1():
        spread(pnk, norh)
        sweep(nor, norh, acc, False, 0, 1)

    def piece2():
        sweep(nor, norh, acc, False, 1, 4)

    def piece3():
        sweep(nor, norh, acc, False, 4, groups)

    def piece4():
        lax.fori_loop(0, height, close, 0)

    share = ch // n1

    def rows_of(m):
        return pl.ds(pl.multiple_of(m * share, share), share)

    def copy1(d):
        m = lax.rem(me1 + d, n1)
        return pltpu.make_async_remote_copy(
            src_ref=pay.at[rows_of(m)],
            dst_ref=rs.at[me1],
            send_sem=r_send.at[d],
            recv_sem=r_recv.at[me1],
            device_id=peer1(m),
            device_id_type=MESH,
        )

    def got1(d):
        m = lax.rem(me1 + d, n1)
        return pltpu.make_async_remote_copy(
            src_ref=pay.at[rows_of(m)],
            dst_ref=rs.at[m],
            send_sem=r_send.at[d],
            recv_sem=r_recv.at[m],
            device_id=peer1(m),
            device_id_type=MESH,
        )

    def exchange(source, slots, me, n, peer, send, recv, meanwhile):
        def put(d):
            m = lax.rem(me + d, n)
            return pltpu.make_async_remote_copy(
                src_ref=source,
                dst_ref=slots.at[me],
                send_sem=send.at[d],
                recv_sem=recv.at[me],
                device_id=peer(m),
                device_id_type=MESH,
            )

        def got(d):
            m = lax.rem(me + d, n)
            return pltpu.make_async_remote_copy(
                src_ref=source,
                dst_ref=slots.at[m],
                send_sem=send.at[d],
                recv_sem=recv.at[m],
                device_id=peer(m),
                device_id_type=MESH,
            )

        def start(d, carry):
            put(d).start()
            return carry

        def arrive(d, carry):
            got(d).wait_recv()
            return carry

        def sent(d, carry):
            put(d).wait_send()
            return carry

        lax.fori_loop(1, n, start, 0)
        slots[me] = source[...]
        meanwhile()
        lax.fori_loop(1, n, arrive, 0)
        return lambda: lax.fori_loop(1, n, sent, 0)

    def start1(d, carry):
        copy1(d).start()
        return carry

    def arrive1(d, carry):
        got1(d).wait_recv()
        return carry

    def sent1(d, carry):
        copy1(d).wait_send()
        return carry

    lax.fori_loop(1, n1, start1, 0)
    rs[me1] = pay[rows_of(me1)]
    piece1()
    lax.fori_loop(1, n1, arrive1, 0)

    def sum_of(slots, n):
        whole = slots[0]
        for k in range(1, n):
            whole = whole + slots[k]
        return whole

    part[...] = sum_of(rs, n1)
    done2 = exchange(part, ex, me2, n2, peer2, e_send, e_recv, piece2)
    part2[...] = sum_of(ex, n2)
    done3 = exchange(part2, ey, me3, n3, peer3, z_send, z_recv, piece3)
    part3[...] = sum_of(ey, n3)
    done4 = exchange(part3, tot, me1, n1, peer1, g_send, g_recv, piece4)
    for k in range(n1):
        pay_out[k * share : (k + 1) * share, :] = tot[k]
    total[...] = jnp.transpose(pay_out[...])

    def sent_pix(d, carry):
        send_pix(at_col(d)).wait_send()
        return carry

    lax.fori_loop(1, nc, sent_pix, 0)
    for copy in u_copies + p_copies:
        copy.wait_send()
    lax.fori_loop(1, n1, sent1, 0)
    done2()
    done3()
    done4()


def per_device(
    place,
    file_pixels,
    patchify_weight,
    patchify_bias,
    norm_gain,
    norm_offset_vector,
    kernel,
    kernel_offset,
    cotangent,
):
    ch, height, breadth = cotangent.shape
    npix = file_pixels.shape[0]
    nc = place["y"] * place["z_hi"] * place["core"]
    n1, n2, n3 = place["x"] * place["core"], place["y"] * place["z_lo"], place["z_hi"]
    share = ch // n1
    wide = nc * lanes
    tall = height + 2 * reach
    plane = (ch, lanes)
    vmem = pl.BlockSpec(memory_space=pltpu.VMEM)
    dma = pltpu.SemaphoreType.DMA
    scratch = [
        pltpu.VMEM((ch, height, lanes), BF16),
        pltpu.VMEM((npix, ch), BF16),
        pltpu.VMEM((sub, ch), F32),
        pltpu.VMEM((side * side, ch), F32),
        pltpu.VMEM((ch, npix), BF16),
        pltpu.VMEM((ch * height, lanes), F32),
        pltpu.VMEM((64, wide), BF16),
        pltpu.VMEM((tall,) + plane, F32),
        pltpu.VMEM((tall,) + plane, F32),
        pltpu.VMEM((tall,) + plane, F32),
        pltpu.VMEM((tall,) + plane, F32),
        pltpu.VMEM((height,) + plane, F32),
        pltpu.VMEM((height,) + plane, F32),
        pltpu.VMEM((side * side + 3,) + plane, F32),
        pltpu.VMEM((side * side,) + plane, F32),
        pltpu.VMEM((4,) + plane, F32),
        pltpu.VMEM((ch, wide), BF16),
        pltpu.VMEM((3, 2) + plane, F32),
        pltpu.VMEM((2 * reach,) + plane, BF16),
        pltpu.VMEM((2, reach) + plane, BF16),
        pltpu.VMEM((2,) + plane, F32),
        pltpu.VMEM((2,) + plane, BF16),
        pltpu.VMEM((6,) + plane, BF16),
        pltpu.VMEM((2, npix, reach * lanes), BF16),
        pltpu.VMEM((2, npix, lanes), BF16),
        pltpu.VMEM((6, npix, lanes), BF16),
        pltpu.VMEM((2,) + plane, F32),
        pltpu.VMEM((2, 3 * side) + plane, F32),
        pltpu.VMEM(plane, F32),
        pltpu.VMEM((n1, share, lanes), F32),
        pltpu.VMEM((share, lanes), F32),
        pltpu.VMEM((n2, share, lanes), F32),
        pltpu.VMEM((share, lanes), F32),
        pltpu.VMEM((n3, share, lanes), F32),
        pltpu.VMEM((share, lanes), F32),
        pltpu.VMEM((n1, share, lanes), F32),
        pltpu.VMEM(plane, F32),
        dma((7,)),
        dma((nc,)),
        dma((nc,)),
        dma(()),
        dma((8,)),
        dma((8,)),
        dma((8,)),
        dma((8,)),
        dma((n1,)),
        dma((n1,)),
        dma((n2,)),
        dma((n2,)),
        dma((n3,)),
        dma((n3,)),
        dma((n1,)),
        dma((n1,)),
    ]
    stem, total = pl.pallas_call(
        functools.partial(body, place),
        out_shape=(
            jax.ShapeDtypeStruct((height,) + plane, BF16),
            jax.ShapeDtypeStruct((lanes, ch), F32),
        ),
        in_specs=[pl.BlockSpec(memory_space=pltpu.HBM)] * 8,
        out_specs=(vmem, vmem),
        scratch_shapes=scratch,
        compiler_params=pltpu.CompilerParams(
            collective_id=0, has_side_effects=True, vmem_limit_bytes=40 << 20
        ),
    )(
        file_pixels.reshape(npix, wide),
        cotangent,
        patchify_weight.T,
        patchify_bias.reshape(1, ch),
        norm_gain.reshape(1, ch),
        norm_offset_vector.reshape(1, ch),
        kernel.T,
        kernel_offset.reshape(1, ch),
    )
    taps_at = 64
    after = taps_at + side * side
    return (
        jnp.transpose(stem, (1, 0, 2)),
        total[0:npix].T,
        total[npix],
        total[after],
        total[after + 1],
        total[taps_at:after].T,
        total[after + 2],
    )


def solution(mesh, place=PLACE):
    return jax.shard_map(
        functools.partial(per_device, place),
        mesh=mesh,
        in_specs=(
            P(None, ("rows", "cols"), None),
            P(),
            P(),
            P(),
            P(),
            P(),
            P(),
            P(None, "rows", "cols"),
        ),
        out_specs=(P(None, "rows", "cols"), P(), P(), P(), P(), P(), P()),
        check_vma=False,
    )
```

```python
import functools
import math

import jax
import jax.numpy as jnp
from jax import lax
from jax.experimental import pallas as pl
from jax.experimental.pallas import tpu as pltpu
from jax.sharding import PartitionSpec as P

MESH = pl.DeviceIdType.MESH
F32 = jnp.float32
BF16 = jnp.bfloat16
norm_eps = 1e-06
side = 7
reach = 3
lanes = 128
sub = 8
PLACE = {"z_lo": 4, "x": 4, "y": 4, "z_hi": 4, "core": 2}


def body(
    place,
    pix,
    cot_in,
    weight_in,
    bias_in,
    gain_in,
    shift_in,
    kernel_in,
    koff_in,
    stem,
    total,
    cot,
    weight_t,
    lines,
    kernel,
    weight,
    cotf,
    pixb,
    up,
    nor,
    norh,
    ng,
    acc,
    kgacc,
    taps,
    cols,
    pgb,
    sums,
    uedge,
    urow,
    upk,
    upack,
    upeer,
    prow,
    ppack,
    ppeer,
    pnk,
    turns,
    pay,
    rs,
    part,
    ex,
    part2,
    ey,
    part3,
    tot,
    pay_out,
    in_sem,
    a_send,
    a_recv,
    own_sem,
    u_send,
    u_recv,
    p_send,
    p_recv,
    r_send,
    r_recv,
    e_send,
    e_recv,
    z_send,
    z_recv,
    g_send,
    g_recv,
):
    nr = place["z_lo"] * place["x"]
    nc = place["y"] * place["z_hi"] * place["core"]
    ch, height = cot.shape[0], cot.shape[1]
    npix = pix.shape[0]
    tall = height + 2 * reach
    groups = ch // sub
    factor = 1.0 / math.sqrt(height * nr * lanes * nc)
    row = lax.axis_index("rows")
    col = lax.axis_index("cols")
    nx, ncore, nzl, ny, nzh = (place[k] for k in ("x", "core", "z_lo", "y", "z_hi"))
    x, zl = lax.rem(row, nx), row // nx
    core = lax.rem(col, ncore)
    zh = lax.rem(col // ncore, nzh)
    y = col // (ncore * nzh)
    lane8 = lax.broadcasted_iota(jnp.int32, (sub, lanes), 1)
    lane = lax.broadcasted_iota(jnp.int32, (ch, lanes), 1)
    lanep = lax.broadcasted_iota(jnp.int32, (npix, lanes), 1)

    def at_row(step):
        return lax.rem(row + step + nr, nr)

    def at_col(step):
        return lax.rem(col + step + nc, nc)

    n1, n2, n3 = nx * ncore, ny * nzl, nzh
    me1, me2, me3 = x * ncore + core, y * nzl + zl, zh

    def peer1(m):
        return (zl * nx + m // ncore, (col - core) + lax.rem(m, ncore))

    def peer2(m):
        return (lax.rem(m, nzl) * nx + x, (m // nzl) * (ncore * nzh) + lax.rem(col, ncore * nzh))

    def peer3(m):
        return (row, y * (ncore * nzh) + m * ncore + core)

    loads = [
        pltpu.make_async_copy(source, target, in_sem.at[at])
        for at, (source, target) in enumerate(
            (
                (cot_in, cot),
                (kernel_in, kernel),
                (weight_in, weight_t),
                (bias_in, lines.at[0:1]),
                (gain_in, lines.at[1:2]),
                (shift_in, lines.at[2:3]),
                (koff_in, lines.at[3:4]),
            )
        )
    ]
    for copy in loads:
        copy.start()

    barrier = pltpu.get_barrier_semaphore()

    def greet(device):
        pl.semaphore_signal(barrier, inc=1, device_id=device, device_id_type=MESH)

    far = sorted(range(nzh), key=lambda d: -min(d, nzh - d))
    near_cols = ny * ncore

    def col_of(dz, e):
        return (
            lax.rem(y + e // ncore, ny) * (ncore * nzh)
            + lax.rem(zh + dz, nzh) * ncore
            + lax.rem(core + lax.rem(e, ncore), ncore)
        )

    def each_col(act):
        for dz in far:

            def one(e, carry, dz=dz):
                act(col_of(dz, e))
                return carry

            lax.fori_loop(1 if dz == 0 else 0, near_cols, one, 0)

    each_col(lambda c: greet((row, c)))
    near = [(dr, dc) for dr in (-1, 1) for dc in (-1, 0, 1)]
    for dr, dc in near:
        greet((at_row(dr), at_col(dc)))

    def greet1(d, carry):
        greet(peer1(lax.rem(me1 + d, n1)))
        return carry

    def greet2(d, carry):
        greet(peer2(lax.rem(me2 + d, n2)))
        return carry

    lax.fori_loop(1, n2, greet2, 0)
    lax.fori_loop(1, n1, greet1, 0)

    def pack(load, mask_lane, shape):
        def step(h, both):
            left, right = both
            v = load(h)
            at = 3 * h
            here = (mask_lane >= at) & (mask_lane < at + 3)
            left = jnp.where(here, pltpu.roll(v, at, 1), left)
            right = jnp.where(here, pltpu.roll(v, at + 3, 1), right)
            return left, right

        zero = jnp.zeros(shape, F32)
        return lax.fori_loop(0, height, step, (zero, zero))

    loads[0].wait()
    for k in range(ch):
        cotf[k * height : (k + 1) * height, :] = cot[k].astype(F32)

    def lift(h, carry):
        up[h + reach] = cotf[pl.ds(h, ch, stride=height), :]
        return carry

    lax.fori_loop(0, height, lift, 0)
    left, right = pack(lambda h: up[h + reach], lane, (ch, lanes))
    upk[0] = left
    upk[1] = right
    upack[0] = left.astype(BF16)
    upack[1] = right.astype(BF16)
    for k in range(reach):
        uedge[k] = up[reach + k].astype(BF16)
        uedge[reach + k] = up[height + k].astype(BF16)

    for copy in loads[1:]:
        copy.wait()
    eye = lax.broadcasted_iota(jnp.int32, (ch, ch), 0) == lax.broadcasted_iota(
        jnp.int32, (ch, ch), 1
    )

    def column(line):
        spot = jnp.where(eye, jnp.broadcast_to(line, (ch, ch)), 0.0)
        return jnp.broadcast_to(jnp.sum(spot, axis=1, keepdims=True), (ch, lanes))

    for at in range(4):
        cols[at] = column(lines[at : at + 1, :])
    weight[...] = jnp.transpose(weight_t[...].astype(F32)).astype(BF16)

    pl.semaphore_wait(barrier, (nc - 1) + len(near) + (n1 - 1) + (n2 - 1))

    def halo_copies(rows_lo, rows_hi, packed, row_dst, pack_dst, send, recv):
        copies = [
            pltpu.make_async_remote_copy(
                src_ref=rows_lo,
                dst_ref=row_dst.at[1],
                send_sem=send.at[0],
                recv_sem=recv.at[1],
                device_id=(at_row(-1), col),
                device_id_type=MESH,
            ),
            pltpu.make_async_remote_copy(
                src_ref=rows_hi,
                dst_ref=row_dst.at[0],
                send_sem=send.at[1],
                recv_sem=recv.at[0],
                device_id=(at_row(1), col),
                device_id_type=MESH,
            ),
        ]
        for which, dc in ((0, -1), (1, 1)):
            for dr in (0, -1, 1):
                slot = (1 - which) * 3 + (1 - dr)
                copies.append(
                    pltpu.make_async_remote_copy(
                        src_ref=packed.at[which],
                        dst_ref=pack_dst.at[slot],
                        send_sem=send.at[2 + slot],
                        recv_sem=recv.at[2 + slot],
                        device_id=(at_row(dr), at_col(dc)),
                        device_id_type=MESH,
                    )
                )
        return copies

    u_copies = halo_copies(
        uedge.at[0:reach], uedge.at[reach : 2 * reach], upack, urow, upeer, u_send, u_recv
    )
    for copy in u_copies:
        copy.start()

    def block(c):
        return pl.ds(pl.multiple_of(c * lanes, lanes), lanes)

    def send_pix(target):
        return pltpu.make_async_remote_copy(
            src_ref=pix.at[:, block(target)],
            dst_ref=pixb.at[0:npix, block(col)],
            send_sem=a_send.at[target],
            recv_sem=a_recv.at[col],
            device_id=(row, target),
            device_id_type=MESH,
        )

    def got_pix(source):
        return pltpu.make_async_remote_copy(
            src_ref=pix.at[:, block(col)],
            dst_ref=pixb.at[0:npix, block(source)],
            send_sem=a_send.at[source],
            recv_sem=a_recv.at[source],
            device_id=(row, source),
            device_id_type=MESH,
        )

    each_col(lambda c: send_pix(c).start())
    own = pltpu.make_async_copy(pix.at[:, block(col)], pixb.at[0:npix, block(col)], own_sem)
    own.start()

    for tap in range(side * side):
        taps[tap] = column(kernel[tap : tap + 1, :])
    extra = pixb.shape[0] - npix
    wide = pixb.shape[1]
    pixb[npix:, :] = jnp.where(
        lax.broadcasted_iota(jnp.int32, (extra, wide), 0) == 0, 1.0, 0.0
    ).astype(BF16)

    def clear(h, carry):
        ng[h] = jnp.zeros((ch, lanes), F32)
        acc[h] = cols[3]
        return carry

    lax.fori_loop(0, height, clear, 0)

    top, bottom = row > 0, row < nr - 1
    west, east = col > 0, col < nc - 1

    def join(peer, which):
        keep = (west, east)[which]
        end = 3 * height
        own = pltpu.roll(peer(3 * which + 1), 9, 1)
        above = pltpu.roll(peer(3 * which), lanes - (end - 9), 1)
        below = pltpu.roll(peer(3 * which + 2), lax.rem(end + 9, lanes), 1)
        first, middle = lane < 9, (lane >= 9) & (lane < end + 9)
        final = (lane >= end + 9) & (lane < end + 18)
        whole = jnp.where(middle & keep, own, 0.0)
        whole = jnp.where(first & (keep & top), above, whole)
        return jnp.where(final & (keep & bottom), below, whole)

    def spread(packed, out):
        lo, hi = packed[0], packed[1]
        for a in range(tall):
            out[a] = jnp.where(
                lane < 64,
                pltpu.roll(hi, (lanes - 3 * a) % lanes, 1),
                pltpu.roll(lo, 125 - 3 * a, 1),
            )

    def turned(j):
        s = reach - j
        return (lane8 >= lanes - s) | (lane8 < -s), lax.rem(s + lanes, lanes)

    outer = [(a, i) for a in range(tall) for i in range(side) if 0 <= a - i < height]
    outer = [(a, i) for a, i in outer if a < reach or a >= height + reach]
    lane16 = lax.broadcasted_iota(jnp.int32, (2 * sub, lanes), 1)
    place3 = lax.rem(lane16, 3)

    def sweep(src, halo, out, flip, first, final):
        inside = range(tall) if halo is not None else range(reach, height + reach)

        def one(step, carry):
            g, j = step // side, lax.rem(step, side)
            gs = pl.ds(pl.multiple_of(g * sub, sub), sub)
            mask, amount = turned(j)
            if flip:
                t = [taps[(side - 1 - i) * side + (side - 1 - j), gs] for i in range(side)]
            else:
                t = [taps[i * side + j, gs] for i in range(side)]
            live = {}
            for a in range(tall):
                if a < height:
                    live[a] = out[a, gs]
                if a in inside:
                    beyond = 0.0 if halo is None else halo[a, gs]
                    v = pltpu.roll(jnp.where(mask, beyond, src[a, gs]), amount, 1)
                    for i in range(side):
                        h = a - i
                        if 0 <= h < height:
                            live[h] = live[h] + t[i] * v
                h = a - (side - 1)
                if h >= 0:
                    out[h, gs] = live.pop(h)
            return carry

        lax.fori_loop(first * side, final * side, one, 0)

    def shifted_rows(src, gs, j):
        s = reach - j
        v = {}
        for a in sorted({a for a, _ in outer}):
            v[a] = src[a, gs]
            if s > 0:
                v[a] = jnp.where(lane16 >= lanes - s, 0.0, v[a])
            if s < 0:
                v[a] = jnp.where(lane16 < -s, 0.0, v[a])
            v[a] = pltpu.roll(v[a], s % lanes, 1)
        return v

    def turn(load):
        for which in range(2):
            pnk[which] = join(load, which)
        for at in range(3 * side):
            turns[0, at] = pltpu.roll(pnk[0], (-at) % lanes, 1)
            turns[1, at] = pltpu.roll(pnk[1], (2 - at) % lanes, 1)

    sweep(up, None, ng, True, 0, groups)
    for copy in u_copies:
        copy.wait_recv()
    for k in range(reach):
        up[k] = jnp.where(top, urow[0, k].astype(F32), 0.0)
        up[height + reach + k] = jnp.where(bottom, urow[1, k].astype(F32), 0.0)
    turn(lambda slot: upeer[slot].astype(F32))
    rims = sorted({a - i for a, i in outer})

    def ng_outer(g, carry):
        gs = pl.ds(pl.multiple_of(g * 2 * sub, 2 * sub), 2 * sub)
        live = {h: ng[h, gs] for h in rims}
        lo = jnp.zeros((2 * sub, lanes), F32)
        hi = jnp.zeros((2 * sub, lanes), F32)
        for j in range(side):
            v = shifted_rows(up, gs, j)
            for i in range(side):
                t = taps[(side - 1 - i) * side + (side - 1 - j), gs]
                for a, tap_row in outer:
                    if tap_row == i:
                        live[a - i] = live[a - i] + t * v[a]
                if j < reach:
                    lo = lo + jnp.where(place3 < reach - j, t * turns[0, 3 * i + j, gs], 0.0)
                if j > reach:
                    hi = hi + jnp.where(
                        place3 >= 2 * reach - j, t * turns[1, 3 * i + j - 4, gs], 0.0
                    )
        for h in rims:
            ng[h, gs] = live[h]
        pnk[0, gs] = lo
        pnk[1, gs] = hi
        return carry

    lax.fori_loop(0, ch // (2 * sub), ng_outer, 0)
    lo, hi = pnk[0], pnk[1]
    for h in range(height):
        ng[h] += jnp.where(
            lane < reach,
            pltpu.roll(lo, (-3 * h) % lanes, 1),
            jnp.where(lane >= lanes - reach, pltpu.roll(hi, (125 - 3 * h) % lanes, 1), 0.0),
        )

    own.wait()

    def embed(pixels):
        patch = jnp.dot(weight[...], pixels, preferred_element_type=F32) + cols[0]
        v = patch.astype(BF16).astype(F32)
        center = v - jnp.mean(v, axis=0, keepdims=True)
        deviation = lax.rsqrt(jnp.mean(center * center, axis=0, keepdims=True) + norm_eps)
        return center * deviation, deviation

    def finish(hat):
        return (hat * cols[1] + cols[2]).astype(BF16).astype(F32)

    sums[...] = jnp.zeros_like(sums)

    def inner(dz, e, both):
        c0 = col_of(dz, ncore * e) - core
        left, right = both
        for k in range(ncore):
            h = c0 + k

            @pl.when(h != col)
            def _(h=h):
                got_pix(h).wait_recv()

        for k in range(ncore):
            h = c0 + k
            pixels = pixb[0:npix, block(h)]
            v = pixels.astype(F32)
            here = (lanep >= 3 * h) & (lanep < 3 * h + 3)
            left = jnp.where(here, pltpu.roll(v, 3 * h, 1), left)
            right = jnp.where(here, pltpu.roll(v, 3 * h + 3, 1), right)
            hat, deviation = embed(pixels)
            nor[h + reach] = finish(hat)
            grad = ng[h] * factor
            sums[0, k] += grad * hat
            sums[1, k] += grad
            sums[2, k] += up[h + reach]
            xgrad = grad * cols[1]
            mean1 = jnp.mean(xgrad, axis=0, keepdims=True)
            mean2 = jnp.mean(xgrad * hat, axis=0, keepdims=True)
            pgb[:, block(h)] = (deviation * (xgrad - mean1 - hat * mean2)).astype(BF16)
        return left, right

    edges = (jnp.zeros((npix, lanes), F32), jnp.zeros((npix, lanes), F32))
    for dz in far[::-1]:
        edges = lax.fori_loop(0, ny, functools.partial(lambda dz, e, b: inner(dz, e, b), dz), edges)
    ppack[0] = edges[0].astype(BF16)
    ppack[1] = edges[1].astype(BF16)
    p_copies = halo_copies(
        pixb.at[0:npix, 0 : reach * lanes],
        pixb.at[0:npix, (height - reach) * lanes : height * lanes],
        ppack,
        prow,
        ppeer,
        p_send,
        p_recv,
    )
    for copy in p_copies:
        copy.start()

    grads = lax.dot_general(
        pgb[...], pixb[...], (((1,), (1,)), ((), ())), preferred_element_type=F32
    )
    pay[...] = jnp.zeros_like(pay)
    pay[:, 0 : pixb.shape[0]] = grads

    def kg_inner(step, carry):
        g, j = step // side, lax.rem(step, side)
        gs = pl.ds(pl.multiple_of(g * sub, sub), sub)
        mask, amount = turned(j)
        sumk = [None] * side
        us = {}
        for a in range(tall - reach):
            if a < height:
                us[a] = up[a + reach, gs]
            if a >= reach:
                v = pltpu.roll(jnp.where(mask, 0.0, nor[a, gs]), amount, 1)
                for i in range(side):
                    h = a - i
                    if 0 <= h < height:
                        term = us[h] * v
                        sumk[i] = term if sumk[i] is None else sumk[i] + term
            us.pop(a - (side - 1), None)
        for i in range(side):
            kgacc[i * side + j, gs] = sumk[i]
        return carry

    lax.fori_loop(0, groups * side, kg_inner, 0)

    for copy in p_copies:
        copy.wait_recv()
    for k in range(reach):
        ks = slice(k * lanes, (k + 1) * lanes)
        nor[k] = jnp.where(top, finish(embed(prow[0, :, ks])[0]), 0.0)
        nor[height + reach + k] = jnp.where(bottom, finish(embed(prow[1, :, ks])[0]), 0.0)
    turn(lambda slot: finish(embed(ppeer[slot])[0]))

    def kg_outer(g, carry):
        gs = pl.ds(pl.multiple_of(g * 2 * sub, 2 * sub), 2 * sub)
        for j in range(side):
            s = reach - j
            v = shifted_rows(nor, gs, j)
            if s > 0:
                edge = jnp.where(place3 < s, upk[0, gs], 0.0)
            if s < 0:
                edge = jnp.where(place3 >= reach + s, upk[1, gs], 0.0)
            for i in range(side):
                whole = kgacc[i * side + j, gs]
                for a, tap_row in outer:
                    if tap_row == i:
                        whole = whole + up[a - i + reach, gs] * v[a]
                if s > 0:
                    whole = whole + edge * turns[0, 3 * i + j, gs]
                if s < 0:
                    whole = whole + edge * turns[1, 3 * i + j - 4, gs]
                kgacc[i * side + j, gs] = whole
        return carry

    lax.fori_loop(0, ch // (2 * sub), kg_outer, 0)
    ones = jnp.ones((lanes, lanes), BF16)
    for at, scale in ((0, 1.0 / factor), (1, 1.0 / factor), (2, 1.0)):
        kgacc[side * side + at] = (sums[at, 0] + sums[at, 1]) * scale
    whole = pay[...]
    for first in range(0, side * side + 3, side):
        count = min(side, side * side + 3 - first)
        value = kgacc[first : first + count].reshape(count * ch, lanes)
        high = value.astype(BF16)
        low = (value - high.astype(F32)).astype(BF16)
        lines_of = jnp.dot(high, ones, preferred_element_type=F32)
        lines_of += jnp.dot(low, ones, preferred_element_type=F32)
        for k in range(count):
            whole = jnp.where(
                lane == 64 + first + k, lines_of[k * ch : (k + 1) * ch] * factor, whole
            )
    pay[...] = whole

    def close(h, carry):
        cotf[pl.ds(h, ch, stride=height), :] = acc[h]
        return carry

    def piece1():
        spread(pnk, norh)
        sweep(nor, norh, acc, False, 0, 1)

    def piece2():
        sweep(nor, norh, acc, False, 1, 4)

    def piece3():
        sweep(nor, norh, acc, False, 4, groups)

    def piece4():
        lax.fori_loop(0, height, close, 0)
        for k in range(ch):
            stem[k] = cotf[k * height : (k + 1) * height, :].astype(BF16)

    share = ch // n1

    def rows_of(m):
        return pl.ds(pl.multiple_of(m * share, share), share)

    def copy1(d):
        m = lax.rem(me1 + d, n1)
        return pltpu.make_async_remote_copy(
            src_ref=pay.at[rows_of(m)],
            dst_ref=rs.at[me1],
            send_sem=r_send.at[d],
            recv_sem=r_recv.at[me1],
            device_id=peer1(m),
            device_id_type=MESH,
        )

    def got1(d):
        m = lax.rem(me1 + d, n1)
        return pltpu.make_async_remote_copy(
            src_ref=pay.at[rows_of(m)],
            dst_ref=rs.at[m],
            send_sem=r_send.at[d],
            recv_sem=r_recv.at[m],
            device_id=peer1(m),
            device_id_type=MESH,
        )

    def exchange(source, slots, me, n, peer, send, recv, meanwhile):
        def put(d):
            m = lax.rem(me + d, n)
            return pltpu.make_async_remote_copy(
                src_ref=source,
                dst_ref=slots.at[me],
                send_sem=send.at[d],
                recv_sem=recv.at[me],
                device_id=peer(m),
                device_id_type=MESH,
            )

        def got(d):
            m = lax.rem(me + d, n)
            return pltpu.make_async_remote_copy(
                src_ref=source,
                dst_ref=slots.at[m],
                send_sem=send.at[d],
                recv_sem=recv.at[m],
                device_id=peer(m),
                device_id_type=MESH,
            )

        def start(d, carry):
            put(d).start()
            return carry

        def arrive(d, carry):
            got(d).wait_recv()
            return carry

        def sent(d, carry):
            put(d).wait_send()
            return carry

        lax.fori_loop(1, n, start, 0)
        slots[me] = source[...]
        meanwhile()
        lax.fori_loop(1, n, arrive, 0)
        return lambda: lax.fori_loop(1, n, sent, 0)

    def start1(d, carry):
        copy1(d).start()
        return carry

    def arrive1(d, carry):
        got1(d).wait_recv()
        return carry

    def sent1(d, carry):
        copy1(d).wait_send()
        return carry

    lax.fori_loop(1, n1, start1, 0)
    rs[me1] = pay[rows_of(me1)]
    piece1()
    lax.fori_loop(1, n1, arrive1, 0)

    def sum_of(slots, n):
        whole = slots[0]
        for k in range(1, n):
            whole = whole + slots[k]
        return whole

    part[...] = sum_of(rs, n1)
    done2 = exchange(part, ex, me2, n2, peer2, e_send, e_recv, piece2)
    part2[...] = sum_of(ex, n2)
    done3 = exchange(part2, ey, me3, n3, peer3, z_send, z_recv, piece3)
    part3[...] = sum_of(ey, n3)
    done4 = exchange(part3, tot, me1, n1, peer1, g_send, g_recv, piece4)
    for k in range(n1):
        pay_out[k * share : (k + 1) * share, :] = tot[k]
    total[...] = jnp.transpose(pay_out[...])

    def sent_pix(d, carry):
        send_pix(at_col(d)).wait_send()
        return carry

    lax.fori_loop(1, nc, sent_pix, 0)
    for copy in u_copies + p_copies:
        copy.wait_send()
    lax.fori_loop(1, n1, sent1, 0)
    done2()
    done3()
    done4()


def per_device(
    place,
    file_pixels,
    patchify_weight,
    patchify_bias,
    norm_gain,
    norm_offset_vector,
    kernel,
    kernel_offset,
    cotangent,
):
    ch, height, breadth = cotangent.shape
    npix = file_pixels.shape[0]
    nc = place["y"] * place["z_hi"] * place["core"]
    n1, n2, n3 = place["x"] * place["core"], place["y"] * place["z_lo"], place["z_hi"]
    share = ch // n1
    wide = nc * lanes
    tall = height + 2 * reach
    plane = (ch, lanes)
    vmem = pl.BlockSpec(memory_space=pltpu.VMEM)
    dma = pltpu.SemaphoreType.DMA
    scratch = [
        pltpu.VMEM((ch, height, lanes), BF16),
        pltpu.VMEM((npix, ch), BF16),
        pltpu.VMEM((sub, ch), F32),
        pltpu.VMEM((side * side, ch), F32),
        pltpu.VMEM((ch, npix), BF16),
        pltpu.VMEM((ch * height, lanes), F32),
        pltpu.VMEM((64, wide), BF16),
        pltpu.VMEM((tall,) + plane, F32),
        pltpu.VMEM((tall,) + plane, F32),
        pltpu.VMEM((tall,) + plane, F32),
        pltpu.VMEM((height,) + plane, F32),
        pltpu.VMEM((height,) + plane, F32),
        pltpu.VMEM((side * side + 3,) + plane, F32),
        pltpu.VMEM((side * side,) + plane, F32),
        pltpu.VMEM((4,) + plane, F32),
        pltpu.VMEM((ch, wide), BF16),
        pltpu.VMEM((3, 2) + plane, F32),
        pltpu.VMEM((2 * reach,) + plane, BF16),
        pltpu.VMEM((2, reach) + plane, BF16),
        pltpu.VMEM((2,) + plane, F32),
        pltpu.VMEM((2,) + plane, BF16),
        pltpu.VMEM((6,) + plane, BF16),
        pltpu.VMEM((2, npix, reach * lanes), BF16),
        pltpu.VMEM((2, npix, lanes), BF16),
        pltpu.VMEM((6, npix, lanes), BF16),
        pltpu.VMEM((2,) + plane, F32),
        pltpu.VMEM((2, 3 * side) + plane, F32),
        pltpu.VMEM(plane, F32),
        pltpu.VMEM((n1, share, lanes), F32),
        pltpu.VMEM((share, lanes), F32),
        pltpu.VMEM((n2, share, lanes), F32),
        pltpu.VMEM((share, lanes), F32),
        pltpu.VMEM((n3, share, lanes), F32),
        pltpu.VMEM((share, lanes), F32),
        pltpu.VMEM((n1, share, lanes), F32),
        pltpu.VMEM(plane, F32),
        dma((7,)),
        dma((nc,)),
        dma((nc,)),
        dma(()),
        dma((8,)),
        dma((8,)),
        dma((8,)),
        dma((8,)),
        dma((n1,)),
        dma((n1,)),
        dma((n2,)),
        dma((n2,)),
        dma((n3,)),
        dma((n3,)),
        dma((n1,)),
        dma((n1,)),
    ]
    stem, total = pl.pallas_call(
        functools.partial(body, place),
        out_shape=(
            jax.ShapeDtypeStruct((ch, height, lanes), BF16),
            jax.ShapeDtypeStruct((lanes, ch), F32),
        ),
        in_specs=[pl.BlockSpec(memory_space=pltpu.HBM)] * 8,
        out_specs=(vmem, vmem),
        scratch_shapes=scratch,
        compiler_params=pltpu.CompilerParams(
            collective_id=0, has_side_effects=True, vmem_limit_bytes=40 << 20
        ),
    )(
        *(
            pltpu.with_memory_space_constraint(value, pltpu.HBM)
            for value in (
                file_pixels.reshape(npix, wide),
                cotangent,
                patchify_weight.T,
                patchify_bias.reshape(1, ch),
                norm_gain.reshape(1, ch),
                norm_offset_vector.reshape(1, ch),
                kernel.T,
                kernel_offset.reshape(1, ch),
            )
        )
    )
    taps_at = 64
    after = taps_at + side * side
    return (
        stem,
        total[0:npix].T,
        total[npix],
        total[after],
        total[after + 1],
        total[taps_at:after].T,
        total[after + 2],
    )


def solution(mesh, place=PLACE):
    return jax.shard_map(
        functools.partial(per_device, place),
        mesh=mesh,
        in_specs=(
            P(None, ("rows", "cols"), None),
            P(),
            P(),
            P(),
            P(),
            P(),
            P(),
            P(None, "rows", "cols"),
        ),
        out_specs=(P(None, "rows", "cols"), P(), P(), P(), P(), P(), P()),
        check_vma=False,
    )
```

```python
import functools
import math

import jax
import jax.numpy as jnp
from jax import lax
from jax.experimental import pallas as pl
from jax.experimental.pallas import tpu as pltpu
from jax.sharding import PartitionSpec as P

MESH = pl.DeviceIdType.MESH
F32 = jnp.float32
BF16 = jnp.bfloat16
norm_eps = 1e-06
side = 7
reach = 3
lanes = 128
sub = 8
PLACE = {"z_lo": 4, "x": 4, "y": 4, "z_hi": 4, "core": 2}


def body(
    place,
    pix,
    cot_in,
    weight_in,
    bias_in,
    gain_in,
    shift_in,
    kernel_in,
    koff_in,
    stem,
    total,
    cot,
    weight_t,
    lines,
    kernel,
    weight,
    cotf,
    pixb,
    up,
    nor,
    norh,
    ng,
    acc,
    kgacc,
    taps,
    cols,
    pgb,
    sums,
    uedge,
    urow,
    upk,
    upack,
    upeer,
    prow,
    ppack,
    ppeer,
    pnk,
    turns,
    pay,
    rs,
    part,
    ex,
    part2,
    ey,
    part3,
    tot,
    pay_out,
    in_sem,
    a_send,
    a_recv,
    own_sem,
    u_send,
    u_recv,
    p_send,
    p_recv,
    r_send,
    r_recv,
    e_send,
    e_recv,
    z_send,
    z_recv,
    g_send,
    g_recv,
):
    nr = place["z_lo"] * place["x"]
    nc = place["y"] * place["z_hi"] * place["core"]
    ch, height = cot.shape[0], cot.shape[1]
    npix = pix.shape[0]
    tall = height + 2 * reach
    groups = ch // sub
    factor = 1.0 / math.sqrt(height * nr * lanes * nc)
    row = lax.axis_index("rows")
    col = lax.axis_index("cols")
    nx, ncore, nzl, ny, nzh = (place[k] for k in ("x", "core", "z_lo", "y", "z_hi"))
    x, zl = lax.rem(row, nx), row // nx
    core = lax.rem(col, ncore)
    zh = lax.rem(col // ncore, nzh)
    y = col // (ncore * nzh)
    lane8 = lax.broadcasted_iota(jnp.int32, (sub, lanes), 1)
    lane = lax.broadcasted_iota(jnp.int32, (ch, lanes), 1)
    lanep = lax.broadcasted_iota(jnp.int32, (npix, lanes), 1)

    def at_row(step):
        return lax.rem(row + step + nr, nr)

    def at_col(step):
        return lax.rem(col + step + nc, nc)

    n1, n2, n3 = nx * ncore, ny * nzl, nzh
    me1, me2, me3 = x * ncore + core, y * nzl + zl, zh

    def peer1(m):
        return (zl * nx + m // ncore, (col - core) + lax.rem(m, ncore))

    def peer2(m):
        return (lax.rem(m, nzl) * nx + x, (m // nzl) * (ncore * nzh) + lax.rem(col, ncore * nzh))

    def peer3(m):
        return (row, y * (ncore * nzh) + m * ncore + core)

    loads = [
        pltpu.make_async_copy(source, target, in_sem.at[at])
        for at, (source, target) in enumerate(
            (
                (cot_in, cot),
                (kernel_in, kernel),
                (weight_in, weight_t),
                (bias_in, lines.at[0:1]),
                (gain_in, lines.at[1:2]),
                (shift_in, lines.at[2:3]),
                (koff_in, lines.at[3:4]),
            )
        )
    ]
    for copy in loads:
        copy.start()

    barrier = pltpu.get_barrier_semaphore()

    def greet(device):
        pl.semaphore_signal(barrier, inc=1, device_id=device, device_id_type=MESH)

    far = sorted(range(nzh), key=lambda d: -min(d, nzh - d))
    near_cols = ny * ncore

    def col_of(dz, e):
        return (
            lax.rem(y + e // ncore, ny) * (ncore * nzh)
            + lax.rem(zh + dz, nzh) * ncore
            + lax.rem(core + lax.rem(e, ncore), ncore)
        )

    def each_col(act):
        for dz in far:

            def one(e, carry, dz=dz):
                act(col_of(dz, e))
                return carry

            lax.fori_loop(1 if dz == 0 else 0, near_cols, one, 0)

    each_col(lambda c: greet((row, c)))
    near = [(dr, dc) for dr in (-1, 1) for dc in (-1, 0, 1)]
    for dr, dc in near:
        greet((at_row(dr), at_col(dc)))

    def greet1(d, carry):
        greet(peer1(lax.rem(me1 + d, n1)))
        return carry

    def greet2(d, carry):
        greet(peer2(lax.rem(me2 + d, n2)))
        return carry

    lax.fori_loop(1, n2, greet2, 0)
    lax.fori_loop(1, n1, greet1, 0)

    loads[0].wait()
    for k in range(ch):
        cotf[k * height : (k + 1) * height, :] = cot[k].astype(F32)

    left = jnp.zeros((ch, lanes), F32)
    right = jnp.zeros((ch, lanes), F32)
    for h in range(height):
        v = cotf[pl.ds(h, ch, stride=height), :]
        up[h + reach] = v
        here = (lane >= 3 * h) & (lane < 3 * h + 3)
        left = jnp.where(here, pltpu.roll(v, 3 * h, 1), left)
        right = jnp.where(here, pltpu.roll(v, 3 * h + 3, 1), right)
    upk[0] = left
    upk[1] = right
    upack[0] = left.astype(BF16)
    upack[1] = right.astype(BF16)
    for k in range(reach):
        uedge[k] = up[reach + k].astype(BF16)
        uedge[reach + k] = up[height + k].astype(BF16)

    for copy in loads[1:]:
        copy.wait()
    eye = lax.broadcasted_iota(jnp.int32, (ch, ch), 0) == lax.broadcasted_iota(
        jnp.int32, (ch, ch), 1
    )

    def column(line):
        spot = jnp.where(eye, jnp.broadcast_to(line, (ch, ch)), 0.0)
        return jnp.broadcast_to(jnp.sum(spot, axis=1, keepdims=True), (ch, lanes))

    for at in range(4):
        cols[at] = column(lines[at : at + 1, :])
    weight[...] = jnp.transpose(weight_t[...].astype(F32)).astype(BF16)

    pl.semaphore_wait(barrier, (nc - 1) + len(near) + (n1 - 1) + (n2 - 1))

    def halo_copies(rows_lo, rows_hi, packed, row_dst, pack_dst, send, recv):
        copies = [
            pltpu.make_async_remote_copy(
                src_ref=rows_lo,
                dst_ref=row_dst.at[1],
                send_sem=send.at[0],
                recv_sem=recv.at[1],
                device_id=(at_row(-1), col),
                device_id_type=MESH,
            ),
            pltpu.make_async_remote_copy(
                src_ref=rows_hi,
                dst_ref=row_dst.at[0],
                send_sem=send.at[1],
                recv_sem=recv.at[0],
                device_id=(at_row(1), col),
                device_id_type=MESH,
            ),
        ]
        for which, dc in ((0, -1), (1, 1)):
            for dr in (0, -1, 1):
                slot = (1 - which) * 3 + (1 - dr)
                copies.append(
                    pltpu.make_async_remote_copy(
                        src_ref=packed.at[which],
                        dst_ref=pack_dst.at[slot],
                        send_sem=send.at[2 + slot],
                        recv_sem=recv.at[2 + slot],
                        device_id=(at_row(dr), at_col(dc)),
                        device_id_type=MESH,
                    )
                )
        return copies

    u_copies = halo_copies(
        uedge.at[0:reach], uedge.at[reach : 2 * reach], upack, urow, upeer, u_send, u_recv
    )
    for copy in u_copies:
        copy.start()

    def block(c):
        return pl.ds(pl.multiple_of(c * lanes, lanes), lanes)

    def send_pix(target):
        return pltpu.make_async_remote_copy(
            src_ref=pix.at[:, block(target)],
            dst_ref=pixb.at[0:npix, block(col)],
            send_sem=a_send.at[target],
            recv_sem=a_recv.at[col],
            device_id=(row, target),
            device_id_type=MESH,
        )

    def got_pix(source):
        return pltpu.make_async_remote_copy(
            src_ref=pix.at[:, block(col)],
            dst_ref=pixb.at[0:npix, block(source)],
            send_sem=a_send.at[source],
            recv_sem=a_recv.at[source],
            device_id=(row, source),
            device_id_type=MESH,
        )

    each_col(lambda c: send_pix(c).start())
    own = pltpu.make_async_copy(pix.at[:, block(col)], pixb.at[0:npix, block(col)], own_sem)
    own.start()

    for tap in range(side * side):
        taps[tap] = column(kernel[tap : tap + 1, :])
    extra = pixb.shape[0] - npix
    wide = pixb.shape[1]
    pixb[npix:, :] = jnp.where(
        lax.broadcasted_iota(jnp.int32, (extra, wide), 0) == 0, 1.0, 0.0
    ).astype(BF16)

    def clear(h, carry):
        ng[h] = jnp.zeros((ch, lanes), F32)
        acc[h] = cols[3]
        return carry

    lax.fori_loop(0, height, clear, 0)

    top, bottom = row > 0, row < nr - 1
    west, east = col > 0, col < nc - 1

    def join(peer, which):
        keep = (west, east)[which]
        end = 3 * height
        own = pltpu.roll(peer(3 * which + 1), 9, 1)
        above = pltpu.roll(peer(3 * which), lanes - (end - 9), 1)
        below = pltpu.roll(peer(3 * which + 2), lax.rem(end + 9, lanes), 1)
        first, middle = lane < 9, (lane >= 9) & (lane < end + 9)
        final = (lane >= end + 9) & (lane < end + 18)
        whole = jnp.where(middle & keep, own, 0.0)
        whole = jnp.where(first & (keep & top), above, whole)
        return jnp.where(final & (keep & bottom), below, whole)

    def spread(packed, out):
        lo, hi = packed[0], packed[1]
        for a in range(tall):
            out[a] = jnp.where(
                lane < 64,
                pltpu.roll(hi, (lanes - 3 * a) % lanes, 1),
                pltpu.roll(lo, 125 - 3 * a, 1),
            )

    def turned(j):
        s = reach - j
        return (lane8 >= lanes - s) | (lane8 < -s), lax.rem(s + lanes, lanes)

    outer = [(a, i) for a in range(tall) for i in range(side) if 0 <= a - i < height]
    outer = [(a, i) for a, i in outer if a < reach or a >= height + reach]
    lane16 = lax.broadcasted_iota(jnp.int32, (2 * sub, lanes), 1)
    place3 = lax.rem(lane16, 3)

    def sweep(src, halo, out, flip, first, final, unroll=1):
        inside = range(tall) if halo is not None else range(reach, height + reach)

        def one(step, carry):
            g, j = step // side, lax.rem(step, side)
            gs = pl.ds(pl.multiple_of(g * sub, sub), sub)
            mask, amount = turned(j)
            if flip:
                t = [taps[(side - 1 - i) * side + (side - 1 - j), gs] for i in range(side)]
            else:
                t = [taps[i * side + j, gs] for i in range(side)]
            live = {}
            for a in range(tall):
                if a < height:
                    live[a] = out[a, gs]
                if a in inside:
                    beyond = 0.0 if halo is None else halo[a, gs]
                    v = pltpu.roll(jnp.where(mask, beyond, src[a, gs]), amount, 1)
                    for i in range(side):
                        h = a - i
                        if 0 <= h < height:
                            live[h] = live[h] + t[i] * v
                h = a - (side - 1)
                if h >= 0:
                    out[h, gs] = live.pop(h)
            return carry

        lax.fori_loop(first * side, final * side, one, 0, unroll=unroll)

    def shifted_rows(src, gs, j):
        s = reach - j
        v = {}
        for a in sorted({a for a, _ in outer}):
            v[a] = src[a, gs]
            if s > 0:
                v[a] = jnp.where(lane16 >= lanes - s, 0.0, v[a])
            if s < 0:
                v[a] = jnp.where(lane16 < -s, 0.0, v[a])
            v[a] = pltpu.roll(v[a], s % lanes, 1)
        return v

    def turn(load):
        for which in range(2):
            pnk[which] = join(load, which)
        for at in range(3 * side):
            turns[0, at] = pltpu.roll(pnk[0], (-at) % lanes, 1)
            turns[1, at] = pltpu.roll(pnk[1], (2 - at) % lanes, 1)

    sweep(up, None, ng, True, 0, groups, 2)
    for copy in u_copies:
        copy.wait_recv()
    for k in range(reach):
        up[k] = jnp.where(top, urow[0, k].astype(F32), 0.0)
        up[height + reach + k] = jnp.where(bottom, urow[1, k].astype(F32), 0.0)
    turn(lambda slot: upeer[slot].astype(F32))
    rims = sorted({a - i for a, i in outer})

    def ng_outer(g, carry):
        gs = pl.ds(pl.multiple_of(g * 2 * sub, 2 * sub), 2 * sub)
        live = {h: ng[h, gs] for h in rims}
        lo = jnp.zeros((2 * sub, lanes), F32)
        hi = jnp.zeros((2 * sub, lanes), F32)
        for j in range(side):
            v = shifted_rows(up, gs, j)
            for i in range(side):
                t = taps[(side - 1 - i) * side + (side - 1 - j), gs]
                for a, tap_row in outer:
                    if tap_row == i:
                        live[a - i] = live[a - i] + t * v[a]
                if j < reach:
                    lo = lo + jnp.where(place3 < reach - j, t * turns[0, 3 * i + j, gs], 0.0)
                if j > reach:
                    hi = hi + jnp.where(
                        place3 >= 2 * reach - j, t * turns[1, 3 * i + j - 4, gs], 0.0
                    )
        for h in rims:
            ng[h, gs] = live[h]
        pnk[0, gs] = lo
        pnk[1, gs] = hi
        return carry

    lax.fori_loop(0, ch // (2 * sub), ng_outer, 0)
    lo, hi = pnk[0], pnk[1]
    for h in range(height):
        ng[h] += jnp.where(
            lane < reach,
            pltpu.roll(lo, (-3 * h) % lanes, 1),
            jnp.where(lane >= lanes - reach, pltpu.roll(hi, (125 - 3 * h) % lanes, 1), 0.0),
        )

    own.wait()

    def embed(pixels):
        patch = jnp.dot(weight[...], pixels, preferred_element_type=F32) + cols[0]
        v = patch.astype(BF16).astype(F32)
        center = v - jnp.mean(v, axis=0, keepdims=True)
        deviation = lax.rsqrt(jnp.mean(center * center, axis=0, keepdims=True) + norm_eps)
        return center * deviation, deviation

    def finish(hat):
        return (hat * cols[1] + cols[2]).astype(BF16).astype(F32)

    sums[...] = jnp.zeros_like(sums)

    def inner(dz, e, both):
        c0 = col_of(dz, ncore * e) - core
        left, right = both
        for k in range(ncore):
            h = c0 + k

            @pl.when(h != col)
            def _(h=h):
                got_pix(h).wait_recv()

        for k in range(ncore):
            h = c0 + k
            pixels = pixb[0:npix, block(h)]
            v = pixels.astype(F32)
            here = (lanep >= 3 * h) & (lanep < 3 * h + 3)
            left = jnp.where(here, pltpu.roll(v, 3 * h, 1), left)
            right = jnp.where(here, pltpu.roll(v, 3 * h + 3, 1), right)
            hat, deviation = embed(pixels)
            nor[h + reach] = finish(hat)
            grad = ng[h] * factor
            sums[0, k] += grad * hat
            sums[1, k] += grad
            sums[2, k] += up[h + reach]
            xgrad = grad * cols[1]
            mean1 = jnp.mean(xgrad, axis=0, keepdims=True)
            mean2 = jnp.mean(xgrad * hat, axis=0, keepdims=True)
            pgb[:, block(h)] = (deviation * (xgrad - mean1 - hat * mean2)).astype(BF16)
        return left, right

    edges = (jnp.zeros((npix, lanes), F32), jnp.zeros((npix, lanes), F32))
    for dz in far[::-1]:
        edges = lax.fori_loop(0, ny, functools.partial(lambda dz, e, b: inner(dz, e, b), dz), edges)
    ppack[0] = edges[0].astype(BF16)
    ppack[1] = edges[1].astype(BF16)
    p_copies = halo_copies(
        pixb.at[0:npix, 0 : reach * lanes],
        pixb.at[0:npix, (height - reach) * lanes : height * lanes],
        ppack,
        prow,
        ppeer,
        p_send,
        p_recv,
    )
    for copy in p_copies:
        copy.start()

    grads = lax.dot_general(
        pgb[...], pixb[...], (((1,), (1,)), ((), ())), preferred_element_type=F32
    )
    pay[...] = jnp.zeros_like(pay)
    pay[:, 0 : pixb.shape[0]] = grads

    def kg_inner(step, carry):
        g, j = step // side, lax.rem(step, side)
        gs = pl.ds(pl.multiple_of(g * sub, sub), sub)
        mask, amount = turned(j)
        sumk = [None] * side
        us = {}
        for a in range(tall - reach):
            if a < height:
                us[a] = up[a + reach, gs]
            if a >= reach:
                v = pltpu.roll(jnp.where(mask, 0.0, nor[a, gs]), amount, 1)
                for i in range(side):
                    h = a - i
                    if 0 <= h < height:
                        term = us[h] * v
                        sumk[i] = term if sumk[i] is None else sumk[i] + term
            us.pop(a - (side - 1), None)
        for i in range(side):
            kgacc[i * side + j, gs] = sumk[i]
        return carry

    lax.fori_loop(0, groups * side, kg_inner, 0, unroll=4)

    for copy in p_copies[:2]:
        copy.wait_recv()
    for k in range(reach):
        ks = slice(k * lanes, (k + 1) * lanes)
        nor[k] = jnp.where(top, finish(embed(prow[0, :, ks])[0]), 0.0)
        nor[height + reach + k] = jnp.where(bottom, finish(embed(prow[1, :, ks])[0]), 0.0)

    def kg_rows(g, carry):
        gs = pl.ds(pl.multiple_of(g * 2 * sub, 2 * sub), 2 * sub)
        for j in range(side):
            v = shifted_rows(nor, gs, j)
            for i in range(side):
                terms = [up[a - i + reach, gs] * v[a] for a, tap_row in outer if tap_row == i]
                if terms:
                    kgacc[i * side + j, gs] += functools.reduce(lambda p, q: p + q, terms)
        return carry

    lax.fori_loop(0, ch // (2 * sub), kg_rows, 0)
    for copy in p_copies[2:]:
        copy.wait_recv()
    turn(lambda slot: finish(embed(ppeer[slot])[0]))
    spot = lax.rem(lane, 3)
    for j in range(side):
        s = reach - j
        if s:
            which = 0 if s > 0 else 1
            edge = jnp.where(spot < s if s > 0 else spot >= reach + s, upk[which], 0.0)
            for i in range(side):
                at = 3 * i + j if s > 0 else 3 * i + j - 4
                kgacc[i * side + j] += edge * turns[which, at]

    ones = jnp.ones((lanes, lanes), BF16)
    for at, scale in ((0, 1.0 / factor), (1, 1.0 / factor), (2, 1.0)):
        kgacc[side * side + at] = (sums[at, 0] + sums[at, 1]) * scale
    whole = pay[...]
    for first in range(0, side * side + 3, side):
        count = min(side, side * side + 3 - first)
        value = kgacc[first : first + count].reshape(count * ch, lanes)
        high = value.astype(BF16)
        low = (value - high.astype(F32)).astype(BF16)
        lines_of = jnp.dot(high, ones, preferred_element_type=F32)
        lines_of += jnp.dot(low, ones, preferred_element_type=F32)
        for k in range(count):
            whole = jnp.where(
                lane == 64 + first + k, lines_of[k * ch : (k + 1) * ch] * factor, whole
            )
    pay[...] = whole

    def close(h, carry):
        cotf[pl.ds(h, ch, stride=height), :] = acc[h]
        return carry

    def piece1():
        spread(pnk, norh)
        sweep(nor, norh, acc, False, 0, 1)

    def piece2():
        sweep(nor, norh, acc, False, 1, 4)

    def piece3():
        sweep(nor, norh, acc, False, 4, groups)

    def piece4():
        lax.fori_loop(0, height, close, 0)
        for k in range(ch):
            stem[k] = cotf[k * height : (k + 1) * height, :].astype(BF16)

    share = ch // n1

    def rows_of(m):
        return pl.ds(pl.multiple_of(m * share, share), share)

    def copy1(d):
        m = lax.rem(me1 + d, n1)
        return pltpu.make_async_remote_copy(
            src_ref=pay.at[rows_of(m)],
            dst_ref=rs.at[me1],
            send_sem=r_send.at[d],
            recv_sem=r_recv.at[me1],
            device_id=peer1(m),
            device_id_type=MESH,
        )

    def got1(d):
        m = lax.rem(me1 + d, n1)
        return pltpu.make_async_remote_copy(
            src_ref=pay.at[rows_of(m)],
            dst_ref=rs.at[m],
            send_sem=r_send.at[d],
            recv_sem=r_recv.at[m],
            device_id=peer1(m),
            device_id_type=MESH,
        )

    def exchange(source, slots, me, n, peer, send, recv, meanwhile):
        def put(d):
            m = lax.rem(me + d, n)
            return pltpu.make_async_remote_copy(
                src_ref=source,
                dst_ref=slots.at[me],
                send_sem=send.at[d],
                recv_sem=recv.at[me],
                device_id=peer(m),
                device_id_type=MESH,
            )

        def got(d):
            m = lax.rem(me + d, n)
            return pltpu.make_async_remote_copy(
                src_ref=source,
                dst_ref=slots.at[m],
                send_sem=send.at[d],
                recv_sem=recv.at[m],
                device_id=peer(m),
                device_id_type=MESH,
            )

        def start(d, carry):
            put(d).start()
            return carry

        def arrive(d, carry):
            got(d).wait_recv()
            return carry

        def sent(d, carry):
            put(d).wait_send()
            return carry

        lax.fori_loop(1, n, start, 0)
        slots[me] = source[...]
        meanwhile()
        lax.fori_loop(1, n, arrive, 0)
        return lambda: lax.fori_loop(1, n, sent, 0)

    def start1(d, carry):
        copy1(d).start()
        return carry

    def arrive1(d, carry):
        got1(d).wait_recv()
        return carry

    def sent1(d, carry):
        copy1(d).wait_send()
        return carry

    lax.fori_loop(1, n1, start1, 0)
    rs[me1] = pay[rows_of(me1)]
    piece1()
    lax.fori_loop(1, n1, arrive1, 0)

    def sum_of(slots, n):
        whole = slots[0]
        for k in range(1, n):
            whole = whole + slots[k]
        return whole

    part[...] = sum_of(rs, n1)
    done2 = exchange(part, ex, me2, n2, peer2, e_send, e_recv, piece2)
    part2[...] = sum_of(ex, n2)
    done3 = exchange(part2, ey, me3, n3, peer3, z_send, z_recv, piece3)
    part3[...] = sum_of(ey, n3)
    done4 = exchange(part3, tot, me1, n1, peer1, g_send, g_recv, piece4)
    for k in range(n1):
        pay_out[k * share : (k + 1) * share, :] = tot[k]
    total[...] = jnp.transpose(pay_out[...])

    def sent_pix(d, carry):
        send_pix(at_col(d)).wait_send()
        return carry

    lax.fori_loop(1, nc, sent_pix, 0)
    for copy in u_copies + p_copies:
        copy.wait_send()
    lax.fori_loop(1, n1, sent1, 0)
    done2()
    done3()
    done4()


def per_device(
    place,
    file_pixels,
    patchify_weight,
    patchify_bias,
    norm_gain,
    norm_offset_vector,
    kernel,
    kernel_offset,
    cotangent,
):
    ch, height, breadth = cotangent.shape
    npix = file_pixels.shape[0]
    nc = place["y"] * place["z_hi"] * place["core"]
    n1, n2, n3 = place["x"] * place["core"], place["y"] * place["z_lo"], place["z_hi"]
    share = ch // n1
    wide = nc * lanes
    tall = height + 2 * reach
    plane = (ch, lanes)
    vmem = pl.BlockSpec(memory_space=pltpu.VMEM)
    dma = pltpu.SemaphoreType.DMA
    scratch = [
        pltpu.VMEM((ch, height, lanes), BF16),
        pltpu.VMEM((npix, ch), BF16),
        pltpu.VMEM((sub, ch), F32),
        pltpu.VMEM((side * side, ch), F32),
        pltpu.VMEM((ch, npix), BF16),
        pltpu.VMEM((ch * height, lanes), F32),
        pltpu.VMEM((64, wide), BF16),
        pltpu.VMEM((tall,) + plane, F32),
        pltpu.VMEM((tall,) + plane, F32),
        pltpu.VMEM((tall,) + plane, F32),
        pltpu.VMEM((height,) + plane, F32),
        pltpu.VMEM((height,) + plane, F32),
        pltpu.VMEM((side * side + 3,) + plane, F32),
        pltpu.VMEM((side * side,) + plane, F32),
        pltpu.VMEM((4,) + plane, F32),
        pltpu.VMEM((ch, wide), BF16),
        pltpu.VMEM((3, 2) + plane, F32),
        pltpu.VMEM((2 * reach,) + plane, BF16),
        pltpu.VMEM((2, reach) + plane, BF16),
        pltpu.VMEM((2,) + plane, F32),
        pltpu.VMEM((2,) + plane, BF16),
        pltpu.VMEM((6,) + plane, BF16),
        pltpu.VMEM((2, npix, reach * lanes), BF16),
        pltpu.VMEM((2, npix, lanes), BF16),
        pltpu.VMEM((6, npix, lanes), BF16),
        pltpu.VMEM((2,) + plane, F32),
        pltpu.VMEM((2, 3 * side) + plane, F32),
        pltpu.VMEM(plane, F32),
        pltpu.VMEM((n1, share, lanes), F32),
        pltpu.VMEM((share, lanes), F32),
        pltpu.VMEM((n2, share, lanes), F32),
        pltpu.VMEM((share, lanes), F32),
        pltpu.VMEM((n3, share, lanes), F32),
        pltpu.VMEM((share, lanes), F32),
        pltpu.VMEM((n1, share, lanes), F32),
        pltpu.VMEM(plane, F32),
        dma((7,)),
        dma((nc,)),
        dma((nc,)),
        dma(()),
        dma((8,)),
        dma((8,)),
        dma((8,)),
        dma((8,)),
        dma((n1,)),
        dma((n1,)),
        dma((n2,)),
        dma((n2,)),
        dma((n3,)),
        dma((n3,)),
        dma((n1,)),
        dma((n1,)),
    ]
    stem, total = pl.pallas_call(
        functools.partial(body, place),
        out_shape=(
            jax.ShapeDtypeStruct((ch, height, lanes), BF16),
            jax.ShapeDtypeStruct((lanes, ch), F32),
        ),
        in_specs=[pl.BlockSpec(memory_space=pltpu.HBM)] * 8,
        out_specs=(vmem, vmem),
        scratch_shapes=scratch,
        compiler_params=pltpu.CompilerParams(
            collective_id=0, has_side_effects=True, vmem_limit_bytes=40 << 20
        ),
    )(
        *(
            pltpu.with_memory_space_constraint(value, pltpu.HBM)
            for value in (
                file_pixels.reshape(npix, wide),
                cotangent,
                patchify_weight.T,
                patchify_bias.reshape(1, ch),
                norm_gain.reshape(1, ch),
                norm_offset_vector.reshape(1, ch),
                kernel.T,
                kernel_offset.reshape(1, ch),
            )
        )
    )
    taps_at = 64
    after = taps_at + side * side
    return (
        stem,
        total[0:npix].T,
        total[npix],
        total[after],
        total[after + 1],
        total[taps_at:after].T,
        total[after + 2],
    )


def solution(mesh, place=PLACE):
    return jax.shard_map(
        functools.partial(per_device, place),
        mesh=mesh,
        in_specs=(
            P(None, ("rows", "cols"), None),
            P(),
            P(),
            P(),
            P(),
            P(),
            P(),
            P(None, "rows", "cols"),
        ),
        out_specs=(P(None, "rows", "cols"), P(), P(), P(), P(), P(), P()),
        check_vma=False,
    )
```

```python
import functools
import math

import jax
import jax.numpy as jnp
from jax import lax
from jax.experimental import pallas as pl
from jax.experimental.pallas import tpu as pltpu
from jax.sharding import PartitionSpec as P

MESH = pl.DeviceIdType.MESH
F32 = jnp.float32
BF16 = jnp.bfloat16
norm_eps = 1e-06
side = 7
reach = 3
lanes = 128
sub = 8
PLACE = {"z_lo": 4, "x": 4, "y": 4, "z_hi": 4, "core": 2}


def body(
    place,
    pix,
    cot_in,
    weight_in,
    bias_in,
    gain_in,
    shift_in,
    kernel_in,
    koff_in,
    stem,
    total,
    cot,
    weight_t,
    lines,
    kernel,
    weight,
    cotf,
    pixb,
    up,
    nor,
    norh,
    xhat,
    inv,
    ng,
    acc,
    kgacc,
    taps,
    cols,
    pgb,
    sums,
    uedge,
    urow,
    upk,
    upack,
    upeer,
    prow,
    ppack,
    ppeer,
    pnk,
    turns,
    pay,
    rs,
    part,
    ex,
    part2,
    ey,
    part3,
    tot,
    pay_out,
    in_sem,
    a_send,
    a_recv,
    own_sem,
    u_send,
    u_recv,
    p_send,
    p_recv,
    r_send,
    r_recv,
    e_send,
    e_recv,
    z_send,
    z_recv,
    g_send,
    g_recv,
):
    nr = place["z_lo"] * place["x"]
    nc = place["y"] * place["z_hi"] * place["core"]
    ch, height = cot.shape[0], cot.shape[1]
    npix = pix.shape[0]
    tall = height + 2 * reach
    groups = ch // sub
    factor = 1.0 / math.sqrt(height * nr * lanes * nc)
    row = lax.axis_index("rows")
    col = lax.axis_index("cols")
    nx, ncore, nzl, ny, nzh = (place[k] for k in ("x", "core", "z_lo", "y", "z_hi"))
    x, zl = lax.rem(row, nx), row // nx
    core = lax.rem(col, ncore)
    zh = lax.rem(col // ncore, nzh)
    y = col // (ncore * nzh)
    lane8 = lax.broadcasted_iota(jnp.int32, (sub, lanes), 1)
    lane = lax.broadcasted_iota(jnp.int32, (ch, lanes), 1)
    lanep = lax.broadcasted_iota(jnp.int32, (npix, lanes), 1)

    def at_row(step):
        return lax.rem(row + step + nr, nr)

    def at_col(step):
        return lax.rem(col + step + nc, nc)

    n1, n2, n3 = nx * ncore, ny * nzl, nzh
    me1, me2, me3 = x * ncore + core, y * nzl + zl, zh

    def peer1(m):
        return (zl * nx + m // ncore, (col - core) + lax.rem(m, ncore))

    def peer2(m):
        return (lax.rem(m, nzl) * nx + x, (m // nzl) * (ncore * nzh) + lax.rem(col, ncore * nzh))

    def peer3(m):
        return (row, y * (ncore * nzh) + m * ncore + core)

    loads = [
        pltpu.make_async_copy(source, target, in_sem.at[at])
        for at, (source, target) in enumerate(
            (
                (cot_in, cot),
                (kernel_in, kernel),
                (weight_in, weight_t),
                (bias_in, lines.at[0:1]),
                (gain_in, lines.at[1:2]),
                (shift_in, lines.at[2:3]),
                (koff_in, lines.at[3:4]),
            )
        )
    ]
    for copy in loads:
        copy.start()

    barrier = pltpu.get_barrier_semaphore()

    def greet(device):
        pl.semaphore_signal(barrier, inc=1, device_id=device, device_id_type=MESH)

    far = sorted(range(nzh), key=lambda d: -min(d, nzh - d))
    near_cols = ny * ncore

    def col_of(dz, e):
        return (
            lax.rem(y + e // ncore, ny) * (ncore * nzh)
            + lax.rem(zh + dz, nzh) * ncore
            + lax.rem(core + lax.rem(e, ncore), ncore)
        )

    def each_col(act):
        for dz in far:

            def one(e, carry, dz=dz):
                act(col_of(dz, e))
                return carry

            lax.fori_loop(1 if dz == 0 else 0, near_cols, one, 0)

    each_col(lambda c: greet((row, c)))
    near = [(dr, dc) for dr in (-1, 1) for dc in (-1, 0, 1)]
    for dr, dc in near:
        greet((at_row(dr), at_col(dc)))

    def greet1(d, carry):
        greet(peer1(lax.rem(me1 + d, n1)))
        return carry

    def greet2(d, carry):
        greet(peer2(lax.rem(me2 + d, n2)))
        return carry

    lax.fori_loop(1, n2, greet2, 0)
    lax.fori_loop(1, n1, greet1, 0)

    loads[0].wait()
    for k in range(ch):
        cotf[k * height : (k + 1) * height, :] = cot[k].astype(F32)

    left = jnp.zeros((ch, lanes), F32)
    right = jnp.zeros((ch, lanes), F32)
    for h in range(height):
        v = cotf[pl.ds(h, ch, stride=height), :]
        up[h + reach] = v
        here = (lane >= 3 * h) & (lane < 3 * h + 3)
        left = jnp.where(here, pltpu.roll(v, 3 * h, 1), left)
        right = jnp.where(here, pltpu.roll(v, 3 * h + 3, 1), right)
    upk[0] = left
    upk[1] = right
    upack[0] = left.astype(BF16)
    upack[1] = right.astype(BF16)
    for k in range(reach):
        uedge[k] = up[reach + k].astype(BF16)
        uedge[reach + k] = up[height + k].astype(BF16)

    for copy in loads[1:]:
        copy.wait()
    eye = lax.broadcasted_iota(jnp.int32, (ch, ch), 0) == lax.broadcasted_iota(
        jnp.int32, (ch, ch), 1
    )

    def column(line):
        spot = jnp.where(eye, jnp.broadcast_to(line, (ch, ch)), 0.0)
        return jnp.broadcast_to(jnp.sum(spot, axis=1, keepdims=True), (ch, lanes))

    for at in range(4):
        cols[at] = column(lines[at : at + 1, :])
    weight[...] = jnp.transpose(weight_t[...].astype(F32)).astype(BF16)

    pl.semaphore_wait(barrier, (nc - 1) + len(near) + (n1 - 1) + (n2 - 1))

    def halo_copies(rows_lo, rows_hi, packed, row_dst, pack_dst, send, recv):
        copies = [
            pltpu.make_async_remote_copy(
                src_ref=rows_lo,
                dst_ref=row_dst.at[1],
                send_sem=send.at[0],
                recv_sem=recv.at[1],
                device_id=(at_row(-1), col),
                device_id_type=MESH,
            ),
            pltpu.make_async_remote_copy(
                src_ref=rows_hi,
                dst_ref=row_dst.at[0],
                send_sem=send.at[1],
                recv_sem=recv.at[0],
                device_id=(at_row(1), col),
                device_id_type=MESH,
            ),
        ]
        for which, dc in ((0, -1), (1, 1)):
            for dr in (0, -1, 1):
                slot = (1 - which) * 3 + (1 - dr)
                copies.append(
                    pltpu.make_async_remote_copy(
                        src_ref=packed.at[which],
                        dst_ref=pack_dst.at[slot],
                        send_sem=send.at[2 + slot],
                        recv_sem=recv.at[2 + slot],
                        device_id=(at_row(dr), at_col(dc)),
                        device_id_type=MESH,
                    )
                )
        return copies

    u_copies = halo_copies(
        uedge.at[0:reach], uedge.at[reach : 2 * reach], upack, urow, upeer, u_send, u_recv
    )
    for copy in u_copies:
        copy.start()

    def block(c):
        return pl.ds(pl.multiple_of(c * lanes, lanes), lanes)

    def send_pix(target):
        return pltpu.make_async_remote_copy(
            src_ref=pix.at[:, block(target)],
            dst_ref=pixb.at[0:npix, block(col)],
            send_sem=a_send.at[target],
            recv_sem=a_recv.at[col],
            device_id=(row, target),
            device_id_type=MESH,
        )

    def got_pix(source):
        return pltpu.make_async_remote_copy(
            src_ref=pix.at[:, block(col)],
            dst_ref=pixb.at[0:npix, block(source)],
            send_sem=a_send.at[source],
            recv_sem=a_recv.at[source],
            device_id=(row, source),
            device_id_type=MESH,
        )

    each_col(lambda c: send_pix(c).start())
    own = pltpu.make_async_copy(pix.at[:, block(col)], pixb.at[0:npix, block(col)], own_sem)
    own.start()

    for tap in range(side * side):
        taps[tap] = column(kernel[tap : tap + 1, :])
    extra = pixb.shape[0] - npix
    wide = pixb.shape[1]
    pixb[npix:, :] = jnp.where(
        lax.broadcasted_iota(jnp.int32, (extra, wide), 0) == 0, 1.0, 0.0
    ).astype(BF16)

    def clear(h, carry):
        ng[h] = jnp.zeros((ch, lanes), F32)
        acc[h] = cols[3]
        return carry

    lax.fori_loop(0, height, clear, 0)

    top, bottom = row > 0, row < nr - 1
    west, east = col > 0, col < nc - 1

    def join(peer, which):
        keep = (west, east)[which]
        end = 3 * height
        own = pltpu.roll(peer(3 * which + 1), 9, 1)
        above = pltpu.roll(peer(3 * which), lanes - (end - 9), 1)
        below = pltpu.roll(peer(3 * which + 2), lax.rem(end + 9, lanes), 1)
        first, middle = lane < 9, (lane >= 9) & (lane < end + 9)
        final = (lane >= end + 9) & (lane < end + 18)
        whole = jnp.where(middle & keep, own, 0.0)
        whole = jnp.where(first & (keep & top), above, whole)
        return jnp.where(final & (keep & bottom), below, whole)

    def spread(packed, out):
        lo, hi = packed[0], packed[1]
        for a in range(tall):
            out[a] = jnp.where(
                lane < 64,
                pltpu.roll(hi, (lanes - 3 * a) % lanes, 1),
                pltpu.roll(lo, 125 - 3 * a, 1),
            )

    def turned(j):
        s = reach - j
        return (lane8 >= lanes - s) | (lane8 < -s), lax.rem(s + lanes, lanes)

    outer = [(a, i) for a in range(tall) for i in range(side) if 0 <= a - i < height]
    outer = [(a, i) for a, i in outer if a < reach or a >= height + reach]
    lane16 = lax.broadcasted_iota(jnp.int32, (2 * sub, lanes), 1)
    place3 = lax.rem(lane16, 3)

    def sweep(src, halo, out, flip, first, final, unroll=1):
        inside = range(tall) if halo is not None else range(reach, height + reach)

        def one(step, carry):
            g, j = step // side, lax.rem(step, side)
            gs = pl.ds(pl.multiple_of(g * sub, sub), sub)
            mask, amount = turned(j)
            if flip:
                t = [taps[(side - 1 - i) * side + (side - 1 - j), gs] for i in range(side)]
            else:
                t = [taps[i * side + j, gs] for i in range(side)]
            live = {}
            for a in range(tall):
                if a < height:
                    live[a] = out[a, gs]
                if a in inside:
                    beyond = 0.0 if halo is None else halo[a, gs]
                    v = pltpu.roll(jnp.where(mask, beyond, src[a, gs]), amount, 1)
                    for i in range(side):
                        h = a - i
                        if 0 <= h < height:
                            live[h] = live[h] + t[i] * v
                h = a - (side - 1)
                if h >= 0:
                    out[h, gs] = live.pop(h)
            return carry

        lax.fori_loop(first * side, final * side, one, 0, unroll=unroll)

    def shifted_rows(src, gs, j):
        s = reach - j
        v = {}
        for a in sorted({a for a, _ in outer}):
            v[a] = src[a, gs]
            if s > 0:
                v[a] = jnp.where(lane16 >= lanes - s, 0.0, v[a])
            if s < 0:
                v[a] = jnp.where(lane16 < -s, 0.0, v[a])
            v[a] = pltpu.roll(v[a], s % lanes, 1)
        return v

    def turn(load):
        for which in range(2):
            pnk[which] = join(load, which)
        for at in range(3 * side):
            turns[0, at] = pltpu.roll(pnk[0], (-at) % lanes, 1)
            turns[1, at] = pltpu.roll(pnk[1], (2 - at) % lanes, 1)

    sweep(up, None, ng, True, 0, groups, 2)
    for copy in u_copies:
        copy.wait_recv()
    for k in range(reach):
        up[k] = jnp.where(top, urow[0, k].astype(F32), 0.0)
        up[height + reach + k] = jnp.where(bottom, urow[1, k].astype(F32), 0.0)
    turn(lambda slot: upeer[slot].astype(F32))
    rims = sorted({a - i for a, i in outer})

    def ng_outer(g, carry):
        gs = pl.ds(pl.multiple_of(g * 2 * sub, 2 * sub), 2 * sub)
        live = {h: ng[h, gs] for h in rims}
        lo = jnp.zeros((2 * sub, lanes), F32)
        hi = jnp.zeros((2 * sub, lanes), F32)
        for j in range(side):
            v = shifted_rows(up, gs, j)
            for i in range(side):
                t = taps[(side - 1 - i) * side + (side - 1 - j), gs]
                for a, tap_row in outer:
                    if tap_row == i:
                        live[a - i] = live[a - i] + t * v[a]
                if j < reach:
                    lo = lo + jnp.where(place3 < reach - j, t * turns[0, 3 * i + j, gs], 0.0)
                if j > reach:
                    hi = hi + jnp.where(
                        place3 >= 2 * reach - j, t * turns[1, 3 * i + j - 4, gs], 0.0
                    )
        for h in rims:
            ng[h, gs] = live[h]
        pnk[0, gs] = lo
        pnk[1, gs] = hi
        return carry

    lax.fori_loop(0, ch // (2 * sub), ng_outer, 0)
    lo, hi = pnk[0], pnk[1]
    for h in range(height):
        ng[h] += jnp.where(
            lane < reach,
            pltpu.roll(lo, (-3 * h) % lanes, 1),
            jnp.where(lane >= lanes - reach, pltpu.roll(hi, (125 - 3 * h) % lanes, 1), 0.0),
        )

    own.wait()

    def embed(pixels):
        patch = jnp.dot(weight[...], pixels, preferred_element_type=F32) + cols[0]
        v = patch.astype(BF16).astype(F32)
        center = v - jnp.mean(v, axis=0, keepdims=True)
        deviation = lax.rsqrt(jnp.mean(center * center, axis=0, keepdims=True) + norm_eps)
        return center * deviation, deviation

    def finish(hat):
        return (hat * cols[1] + cols[2]).astype(BF16).astype(F32)

    sums[...] = jnp.zeros_like(sums)

    def inner(dz, e, both):
        c0 = col_of(dz, ncore * e) - core
        left, right = both
        for k in range(ncore):
            h = c0 + k

            @pl.when(h != col)
            def _(h=h):
                got_pix(h).wait_recv()

        for k in range(ncore):
            h = c0 + k
            pixels = pixb[0:npix, block(h)]
            v = pixels.astype(F32)
            here = (lanep >= 3 * h) & (lanep < 3 * h + 3)
            left = jnp.where(here, pltpu.roll(v, 3 * h, 1), left)
            right = jnp.where(here, pltpu.roll(v, 3 * h + 3, 1), right)
            hat, deviation = embed(pixels)
            nor[h + reach] = finish(hat)
            xhat[h] = hat
            inv[h] = jnp.broadcast_to(deviation, (sub, lanes))
        return left, right

    edges = (jnp.zeros((npix, lanes), F32), jnp.zeros((npix, lanes), F32))
    for dz in far[::-1]:
        edges = lax.fori_loop(0, ny, functools.partial(lambda dz, e, b: inner(dz, e, b), dz), edges)
    ppack[0] = edges[0].astype(BF16)
    ppack[1] = edges[1].astype(BF16)
    p_copies = halo_copies(
        pixb.at[0:npix, 0 : reach * lanes],
        pixb.at[0:npix, (height - reach) * lanes : height * lanes],
        ppack,
        prow,
        ppeer,
        p_send,
        p_recv,
    )
    for copy in p_copies:
        copy.start()

    def inner_back(pair, carry):
        for k in range(2):
            h = 2 * pair + k
            hat, deviation = xhat[h], inv[h, 0:1]
            grad = ng[h] * factor
            sums[0, k] += grad * hat
            sums[1, k] += grad
            sums[2, k] += up[h + reach]
            xgrad = grad * cols[1]
            mean1 = jnp.mean(xgrad, axis=0, keepdims=True)
            mean2 = jnp.mean(xgrad * hat, axis=0, keepdims=True)
            pgb[:, block(h)] = (deviation * (xgrad - mean1 - hat * mean2)).astype(BF16)
        return carry

    lax.fori_loop(0, height // 2, inner_back, 0)
    grads = lax.dot_general(
        pgb[...], pixb[...], (((1,), (1,)), ((), ())), preferred_element_type=F32
    )
    pay[...] = jnp.zeros_like(pay)
    pay[:, 0 : pixb.shape[0]] = grads

    def kg_inner(step, carry):
        g, j = step // side, lax.rem(step, side)
        gs = pl.ds(pl.multiple_of(g * sub, sub), sub)
        mask, amount = turned(j)
        sumk = [None] * side
        us = {}
        for a in range(tall - reach):
            if a < height:
                us[a] = up[a + reach, gs]
            if a >= reach:
                v = pltpu.roll(jnp.where(mask, 0.0, nor[a, gs]), amount, 1)
                for i in range(side):
                    h = a - i
                    if 0 <= h < height:
                        term = us[h] * v
                        sumk[i] = term if sumk[i] is None else sumk[i] + term
            us.pop(a - (side - 1), None)
        for i in range(side):
            kgacc[i * side + j, gs] = sumk[i]
        return carry

    lax.fori_loop(0, groups * side, kg_inner, 0, unroll=4)

    for copy in p_copies[:2]:
        copy.wait_recv()
    for k in range(reach):
        ks = slice(k * lanes, (k + 1) * lanes)
        nor[k] = jnp.where(top, finish(embed(prow[0, :, ks])[0]), 0.0)
        nor[height + reach + k] = jnp.where(bottom, finish(embed(prow[1, :, ks])[0]), 0.0)

    def kg_rows(g, carry):
        gs = pl.ds(pl.multiple_of(g * 2 * sub, 2 * sub), 2 * sub)
        for j in range(side):
            v = shifted_rows(nor, gs, j)
            for i in range(side):
                terms = [up[a - i + reach, gs] * v[a] for a, tap_row in outer if tap_row == i]
                if terms:
                    kgacc[i * side + j, gs] += functools.reduce(lambda p, q: p + q, terms)
        return carry

    lax.fori_loop(0, ch // (2 * sub), kg_rows, 0)
    for copy in p_copies[2:]:
        copy.wait_recv()
    turn(lambda slot: finish(embed(ppeer[slot])[0]))
    spot = lax.rem(lane, 3)
    for j in range(side):
        s = reach - j
        if s:
            which = 0 if s > 0 else 1
            edge = jnp.where(spot < s if s > 0 else spot >= reach + s, upk[which], 0.0)
            for i in range(side):
                at = 3 * i + j if s > 0 else 3 * i + j - 4
                kgacc[i * side + j] += edge * turns[which, at]

    ones = jnp.ones((lanes, lanes), BF16)
    for at, scale in ((0, 1.0 / factor), (1, 1.0 / factor), (2, 1.0)):
        kgacc[side * side + at] = (sums[at, 0] + sums[at, 1]) * scale
    whole = pay[...]
    for first in range(0, side * side + 3, side):
        count = min(side, side * side + 3 - first)
        value = kgacc[first : first + count].reshape(count * ch, lanes)
        high = value.astype(BF16)
        low = (value - high.astype(F32)).astype(BF16)
        lines_of = jnp.dot(high, ones, preferred_element_type=F32)
        lines_of += jnp.dot(low, ones, preferred_element_type=F32)
        for k in range(count):
            whole = jnp.where(
                lane == 64 + first + k, lines_of[k * ch : (k + 1) * ch] * factor, whole
            )
    pay[...] = whole

    def close(h, carry):
        cotf[pl.ds(h, ch, stride=height), :] = acc[h]
        return carry

    def piece1():
        spread(pnk, norh)
        sweep(nor, norh, acc, False, 0, 1)

    def piece2():
        sweep(nor, norh, acc, False, 1, 4)

    def piece3():
        sweep(nor, norh, acc, False, 4, groups)

    def piece4():
        lax.fori_loop(0, height, close, 0)
        for k in range(ch):
            stem[k] = cotf[k * height : (k + 1) * height, :].astype(BF16)

    share = ch // n1

    def rows_of(m):
        return pl.ds(pl.multiple_of(m * share, share), share)

    def copy1(d):
        m = lax.rem(me1 + d, n1)
        return pltpu.make_async_remote_copy(
            src_ref=pay.at[rows_of(m)],
            dst_ref=rs.at[me1],
            send_sem=r_send.at[d],
            recv_sem=r_recv.at[me1],
            device_id=peer1(m),
            device_id_type=MESH,
        )

    def got1(d):
        m = lax.rem(me1 + d, n1)
        return pltpu.make_async_remote_copy(
            src_ref=pay.at[rows_of(m)],
            dst_ref=rs.at[m],
            send_sem=r_send.at[d],
            recv_sem=r_recv.at[m],
            device_id=peer1(m),
            device_id_type=MESH,
        )

    def exchange(source, slots, me, n, peer, send, recv, meanwhile):
        def put(d):
            m = lax.rem(me + d, n)
            return pltpu.make_async_remote_copy(
                src_ref=source,
                dst_ref=slots.at[me],
                send_sem=send.at[d],
                recv_sem=recv.at[me],
                device_id=peer(m),
                device_id_type=MESH,
            )

        def got(d):
            m = lax.rem(me + d, n)
            return pltpu.make_async_remote_copy(
                src_ref=source,
                dst_ref=slots.at[m],
                send_sem=send.at[d],
                recv_sem=recv.at[m],
                device_id=peer(m),
                device_id_type=MESH,
            )

        def start(d, carry):
            put(d).start()
            return carry

        def arrive(d, carry):
            got(d).wait_recv()
            return carry

        def sent(d, carry):
            put(d).wait_send()
            return carry

        lax.fori_loop(1, n, start, 0)
        slots[me] = source[...]
        meanwhile()
        lax.fori_loop(1, n, arrive, 0)
        return lambda: lax.fori_loop(1, n, sent, 0)

    def start1(d, carry):
        copy1(d).start()
        return carry

    def arrive1(d, carry):
        got1(d).wait_recv()
        return carry

    def sent1(d, carry):
        copy1(d).wait_send()
        return carry

    lax.fori_loop(1, n1, start1, 0)
    rs[me1] = pay[rows_of(me1)]
    piece1()
    lax.fori_loop(1, n1, arrive1, 0)

    def sum_of(slots, n):
        whole = slots[0]
        for k in range(1, n):
            whole = whole + slots[k]
        return whole

    part[...] = sum_of(rs, n1)
    done2 = exchange(part, ex, me2, n2, peer2, e_send, e_recv, piece2)
    part2[...] = sum_of(ex, n2)
    done3 = exchange(part2, ey, me3, n3, peer3, z_send, z_recv, piece3)
    part3[...] = sum_of(ey, n3)
    done4 = exchange(part3, tot, me1, n1, peer1, g_send, g_recv, piece4)
    for k in range(n1):
        pay_out[k * share : (k + 1) * share, :] = tot[k]
    total[...] = jnp.transpose(pay_out[...])

    def sent_pix(d, carry):
        send_pix(at_col(d)).wait_send()
        return carry

    lax.fori_loop(1, nc, sent_pix, 0)
    for copy in u_copies + p_copies:
        copy.wait_send()
    lax.fori_loop(1, n1, sent1, 0)
    done2()
    done3()
    done4()


def per_device(
    place,
    file_pixels,
    patchify_weight,
    patchify_bias,
    norm_gain,
    norm_offset_vector,
    kernel,
    kernel_offset,
    cotangent,
):
    ch, height, breadth = cotangent.shape
    npix = file_pixels.shape[0]
    nc = place["y"] * place["z_hi"] * place["core"]
    n1, n2, n3 = place["x"] * place["core"], place["y"] * place["z_lo"], place["z_hi"]
    share = ch // n1
    wide = nc * lanes
    tall = height + 2 * reach
    plane = (ch, lanes)
    vmem = pl.BlockSpec(memory_space=pltpu.VMEM)
    dma = pltpu.SemaphoreType.DMA
    scratch = [
        pltpu.VMEM((ch, height, lanes), BF16),
        pltpu.VMEM((npix, ch), BF16),
        pltpu.VMEM((sub, ch), F32),
        pltpu.VMEM((side * side, ch), F32),
        pltpu.VMEM((ch, npix), BF16),
        pltpu.VMEM((ch * height, lanes), F32),
        pltpu.VMEM((64, wide), BF16),
        pltpu.VMEM((tall,) + plane, F32),
        pltpu.VMEM((tall,) + plane, F32),
        pltpu.VMEM((tall,) + plane, F32),
        pltpu.VMEM((height,) + plane, F32),
        pltpu.VMEM((height, sub, lanes), F32),
        pltpu.VMEM((height,) + plane, F32),
        pltpu.VMEM((height,) + plane, F32),
        pltpu.VMEM((side * side + 3,) + plane, F32),
        pltpu.VMEM((side * side,) + plane, F32),
        pltpu.VMEM((4,) + plane, F32),
        pltpu.VMEM((ch, wide), BF16),
        pltpu.VMEM((3, 2) + plane, F32),
        pltpu.VMEM((2 * reach,) + plane, BF16),
        pltpu.VMEM((2, reach) + plane, BF16),
        pltpu.VMEM((2,) + plane, F32),
        pltpu.VMEM((2,) + plane, BF16),
        pltpu.VMEM((6,) + plane, BF16),
        pltpu.VMEM((2, npix, reach * lanes), BF16),
        pltpu.VMEM((2, npix, lanes), BF16),
        pltpu.VMEM((6, npix, lanes), BF16),
        pltpu.VMEM((2,) + plane, F32),
        pltpu.VMEM((2, 3 * side) + plane, F32),
        pltpu.VMEM(plane, F32),
        pltpu.VMEM((n1, share, lanes), F32),
        pltpu.VMEM((share, lanes), F32),
        pltpu.VMEM((n2, share, lanes), F32),
        pltpu.VMEM((share, lanes), F32),
        pltpu.VMEM((n3, share, lanes), F32),
        pltpu.VMEM((share, lanes), F32),
        pltpu.VMEM((n1, share, lanes), F32),
        pltpu.VMEM(plane, F32),
        dma((7,)),
        dma((nc,)),
        dma((nc,)),
        dma(()),
        dma((8,)),
        dma((8,)),
        dma((8,)),
        dma((8,)),
        dma((n1,)),
        dma((n1,)),
        dma((n2,)),
        dma((n2,)),
        dma((n3,)),
        dma((n3,)),
        dma((n1,)),
        dma((n1,)),
    ]
    stem, total = pl.pallas_call(
        functools.partial(body, place),
        out_shape=(
            jax.ShapeDtypeStruct((ch, height, lanes), BF16),
            jax.ShapeDtypeStruct((lanes, ch), F32),
        ),
        in_specs=[pl.BlockSpec(memory_space=pltpu.HBM)] * 8,
        out_specs=(vmem, vmem),
        scratch_shapes=scratch,
        compiler_params=pltpu.CompilerParams(
            collective_id=0, has_side_effects=True, vmem_limit_bytes=40 << 20
        ),
    )(
        *(
            pltpu.with_memory_space_constraint(value, pltpu.HBM)
            for value in (
                file_pixels.reshape(npix, wide),
                cotangent,
                patchify_weight.T,
                patchify_bias.reshape(1, ch),
                norm_gain.reshape(1, ch),
                norm_offset_vector.reshape(1, ch),
                kernel.T,
                kernel_offset.reshape(1, ch),
            )
        )
    )
    taps_at = 64
    after = taps_at + side * side
    return (
        stem,
        total[0:npix].T,
        total[npix],
        total[after],
        total[after + 1],
        total[taps_at:after].T,
        total[after + 2],
    )


def solution(mesh, place=PLACE):
    return jax.shard_map(
        functools.partial(per_device, place),
        mesh=mesh,
        in_specs=(
            P(None, ("rows", "cols"), None),
            P(),
            P(),
            P(),
            P(),
            P(),
            P(),
            P(None, "rows", "cols"),
        ),
        out_specs=(P(None, "rows", "cols"), P(), P(), P(), P(), P(), P()),
        check_vma=False,
    )
```
